32 devices in a mesh: dp: 4 (over z), section: 2 (over core), ctx: 4 (over y, x).
Axes of the slice: x: 2, y: 2, z: 4, core: 2. Of those that a mesh axis runs over, the one named last changes fastest.
Arguments:
- features: bfloat16 [2, 4096, 8192], P('section', 'ctx', 'dp'), may hold values from -6 to 6
- queries: bfloat16 [2, 4096, 8192], P('section', 'ctx', 'dp'), may hold values from -6 to 6
- keys: bfloat16 [2, 4096, 1024], P('section', 'ctx', 'dp'), may hold values from -6 to 6
- values: bfloat16 [2, 4096, 1024], P('section', 'ctx', 'dp'), may hold values from -6 to 6
- attn_out: bfloat16 [2, 4096, 8192], P('section', 'ctx', 'dp'), may hold values from -4 to 4
- out_grad: bfloat16 [2, 4096, 8192], P('section', 'ctx', 'dp'), may hold values from -6 to 6
- lse: float32 [2, 64, 4096], P('section', 'dp', 'ctx'), as said below
- doc_starts: int32 [2, 65], P('section'), may hold values from 0 to 4096, as said below
- key_blocks: int32 [2, 32, 17], P('section', 'ctx'), may hold values from -1 to 31, as said below
Outputs:
- query_grad: bfloat16 [2, 4096, 8192], P('section', 'ctx', 'dp')
- key_grad: bfloat16 [2, 4096, 1024], P('section', 'ctx', 'dp')
- value_grad: bfloat16 [2, 4096, 1024], P('section', 'ctx', 'dp')
- value_weight_grad: float32 [2, 8192, 1024], P('section', ('dp', 'ctx'))
The draws below stay inside these ranges and needn't reach their ends.
Inputs may be any that keep to these rules, and one draw needn't show every extreme that they name: `doc_starts`: each row lists the first token of each document of one sequence, rising from 0; entries after the last document equal 4096. Every document has 64 to 2049 tokens, except the last, which the sequence's end may cut shorter; one of the first two documents of every sequence has exactly 2049 tokens. `key_blocks`: row b of a section (query block b of 128 tokens) lists in rising order the key blocks from the block holding the start of the document of block b's first token up to b itself, then -1 in the remaining entries. Every section has a row with all 17 entries used. `lse`: Non-negative.
All inputs are finite; a program needn't handle non-finite values.
Results may differ from the reference program's by a relative error of at most 0.0065.
Values may be sent and summed in bfloat16 or wider, within the bound.
A program may use at most 128 MiB of HBM per device.

```python
import jax
import jax.numpy as jnp
from jax import lax

DW = 8192
QH = 64
KVH = 8
HD = 128
DOC_LEAST = 64
QW = 8192
KVW = 1024
SECTIONS = 2
SEQ = 4096
NBLK = 32
KMAX = 17
DOC_MOST = 2049
DOC_CAP = 65


def doc_layout(key):
    base_key = jax.random.fold_in(key, 7)
    seq_keys = jax.random.split(base_key, SECTIONS)

    def one_sequence(seq_key):
        len_key, flag_key, first_key = jax.random.split(seq_key, 3)
        lengths = jax.random.randint(len_key, (DOC_CAP,), DOC_LEAST, DOC_MOST + 1)
        forced_second = jax.random.randint(flag_key, (), 0, 2)
        first_length = jax.random.randint(first_key, (), DOC_LEAST, min(DOC_MOST, SEQ - DOC_MOST) + 1)
        lengths = lengths.at[0].set(jnp.where(forced_second == 1, first_length, DOC_MOST))
        lengths = lengths.at[1].set(jnp.where(forced_second == 1, DOC_MOST, lengths[1]))
        doc_ends = jnp.cumsum(lengths).astype(jnp.int32)
        starts = jnp.concatenate([jnp.zeros((1,), jnp.int32), doc_ends[:-1]])
        return jnp.minimum(starts, SEQ).astype(jnp.int32)
    return jax.vmap(one_sequence)(seq_keys).reshape(SECTIONS, DOC_CAP)


def begin_of_doc(starts, positions):
    hits = starts[:, None, :] <= positions[None, :, None]
    return jnp.max(jnp.where(hits, starts[:, None, :], 0), axis=-1)


def draw_doc_starts(key, part):
    return doc_layout(key)


def draw_key_blocks(key, part):
    starts = doc_layout(key)
    block_ids = jnp.arange(NBLK, dtype=jnp.int32)
    doc_begin = begin_of_doc(starts, block_ids * 128)
    entries = (doc_begin // 128)[..., None] + jnp.arange(KMAX, dtype=jnp.int32)
    listed = jnp.where(entries <= block_ids[None, :, None], entries, -1)
    return listed.reshape(SECTIONS, NBLK, KMAX).astype(jnp.int32)


def draw_lse(key, part):
    starts = doc_layout(key)
    positions = jnp.arange(SEQ, dtype=jnp.int32)
    doc_begin = begin_of_doc(starts, positions)
    visible = (positions[None, :] - doc_begin + 1).astype(jnp.float32)
    base_part = jnp.log(visible).reshape(SECTIONS, 1, SEQ)
    noise_key = jax.random.fold_in(key, 11)
    offset = jax.random.uniform(noise_key, (SECTIONS, QH, SEQ), jnp.float32, 0.3, 0.8)
    return (base_part + offset).astype(jnp.float32)


def spiked(values, rng, source, target, shards_of, factor):
    owner, partner = [(jnp.arange(values.shape[dim]) // (values.shape[dim] // shards_of)).reshape([-1 if axis == dim else 1 for axis in range(values.ndim)]) for dim in (source, target)]
    chosen = jax.random.permutation(rng, shards_of)[partner]
    strong = (owner == chosen) | (owner == (partner + shards_of // 2) % shards_of)
    return jnp.where(strong, factor * values, values)


def block_levels(key, dims, pieces, least, high):
    gain = 1.0
    for axis_at, blocks in pieces:
        draws = jax.random.uniform(jax.random.fold_in(jax.random.fold_in(key, 6), axis_at), (blocks,), jnp.float32, least / len(pieces), high / len(pieces))
        gain = gain * jnp.repeat(jnp.exp(draws), dims[axis_at] // blocks).reshape((-1,) + (1,) * (len(dims) - 1 - axis_at))
    return gain


def scatter_about(key, shape, scale, bound, cuts=(), kind=jnp.bfloat16):
    values = jax.random.normal(key, shape, jnp.float32) * scale
    if len(cuts) > 0:
        values = block_levels(key, shape, cuts, -0.22, 0.18) * values
    return jnp.clip(values, min=-bound, max=bound).astype(kind)


def gaussian_with(key, extent, deviation, limit, pieces, heavy, held_as=jnp.bfloat16):
    values = deviation * jax.random.normal(key, extent, jnp.float32)
    if pieces:
        values = values * block_levels(key, extent, pieces, -0.22, 0.18)
    return jnp.clip(spiked(values, jax.random.fold_in(key, 3), *heavy), -limit, limit).astype(held_as)


def setup_inputs(seed: int = 0) -> dict:
    streams_of = jax.random.split(jax.random.key(seed), 10)
    features = gaussian_with(streams_of[0], (SECTIONS, SEQ, DW), 1.0, 6.0, ((0, 2), (1, 4), (2, 4)), (1, 2, 4, 2.0))
    queries = scatter_about(streams_of[1], (SECTIONS, SEQ, QW), 1.0, 6.0, ((0, 2), (1, 4), (2, 4)))
    keys = scatter_about(streams_of[2], (SECTIONS, SEQ, KVW), 1.0, 6.0, ((0, 2), (1, 4), (2, 4)))
    values = scatter_about(streams_of[3], (SECTIONS, SEQ, KVW), 1.0, 6.0, ((0, 2), (1, 4), (2, 4)))
    attn_out = scatter_about(streams_of[4], (SECTIONS, SEQ, QW), 0.3, 4.0, ((0, 2), (1, 4), (2, 4)))
    out_grad = scatter_about(streams_of[5], (SECTIONS, SEQ, QW), 1.0, 6.0, ((0, 2), (1, 4), (2, 4)))
    lse = draw_lse(jax.random.fold_in(streams_of[9], 71), 0)
    doc_starts = draw_doc_starts(jax.random.fold_in(streams_of[9], 71), 0)
    key_blocks = draw_key_blocks(jax.random.fold_in(streams_of[9], 71), 0)
    return {"features": features, "queries": queries, "keys": keys, "values": values, "attn_out": attn_out, "out_grad": out_grad, "lse": lse, "doc_starts": doc_starts, "key_blocks": key_blocks}


def doc_index(starts, positions):
    return jnp.sum((starts[None, :] <= positions[:, None]).astype(jnp.int32), axis=1) - 1


def head_grads(inputs):
    query_h, key_h, value_h, output_h, grad_h, lse_h, starts, block_list = inputs
    group_size = QH // KVH
    score_scale = HD ** -0.5
    positions = jnp.arange(SEQ, dtype=jnp.int32)
    docs = doc_index(starts, positions)
    query_tiles = query_h.astype(jnp.float32).reshape(NBLK, 128, group_size, HD)
    grad_tiles = grad_h.astype(jnp.float32).reshape(NBLK, 128, group_size, HD)
    output_tiles = output_h.astype(jnp.float32).reshape(NBLK, 128, group_size, HD)
    key_tiles = key_h.astype(jnp.float32).reshape(NBLK, 128, HD)
    value_tiles = value_h.astype(jnp.float32).reshape(NBLK, 128, HD)
    row_delta = jnp.transpose(jnp.sum(grad_tiles * output_tiles, axis=-1), (0, 2, 1))
    lse_tiles = jnp.transpose(lse_h.reshape(group_size, NBLK, 128), (1, 0, 2))
    doc_tiles = docs.reshape(NBLK, 128)
    pos_tiles = positions.reshape(NBLK, 128)
    grad_query = jnp.zeros((NBLK, 128, group_size, HD), jnp.float32)
    grad_key = jnp.zeros((NBLK, 128, HD), jnp.float32)
    grad_value = jnp.zeros((NBLK, 128, HD), jnp.float32)
    for entry_idx in range(KMAX):
        chosen = block_list[:, entry_idx]
        valid_rows = chosen >= 0
        picked = jnp.maximum(chosen, 0).astype(jnp.int32)
        key_sel = key_tiles[picked]
        value_sel = value_tiles[picked]
        allowed = valid_rows[:, None, None] & (doc_tiles[:, :, None] == doc_tiles[picked][:, None, :]) & (pos_tiles[:, :, None] >= pos_tiles[picked][:, None, :])
        scores = jnp.einsum('bird,bjd->brij', query_tiles, key_sel) * score_scale
        prob_full = jnp.where(allowed[:, None], jnp.exp(scores - lse_tiles[..., None]), 0.0)
        prob_half = lax.optimization_barrier(prob_full.astype(jnp.bfloat16)).astype(jnp.float32)
        dprobs = jnp.einsum('bird,bjd->brij', grad_tiles, value_sel)
        dscores = prob_full * (dprobs - row_delta[..., None]) * score_scale
        dscores = lax.optimization_barrier(dscores.astype(jnp.bfloat16)).astype(jnp.float32)
        grad_query = grad_query + jnp.einsum('brij,bjd->bird', dscores, key_sel)
        grad_key = grad_key.at[picked].add(jnp.einsum('brij,bird->bjd', dscores, query_tiles))
        grad_value = grad_value.at[picked].add(jnp.einsum('brij,bird->bjd', prob_half, grad_tiles))
    return (grad_query.reshape(SEQ, group_size * HD).astype(jnp.bfloat16),
            grad_key.reshape(SEQ, HD).astype(jnp.bfloat16),
            grad_value.reshape(SEQ, HD).astype(jnp.bfloat16))


def reference(features, queries, keys, values, attn_out, out_grad, lse, doc_starts, key_blocks):
    group_size = QH // KVH
    item_count = SECTIONS * KVH

    def split_query(array):
        return jnp.transpose(array.reshape(SECTIONS, SEQ, KVH, group_size, HD), (0, 2, 1, 3, 4)).reshape(item_count, SEQ, group_size, HD)

    def split_key(array):
        return jnp.transpose(array.reshape(SECTIONS, SEQ, KVH, HD), (0, 2, 1, 3)).reshape(item_count, SEQ, HD)

    starts_all = jnp.broadcast_to(doc_starts[:, None, :], (SECTIONS, KVH, DOC_CAP)).reshape(item_count, DOC_CAP)
    blocks_all = jnp.broadcast_to(key_blocks[:, None, :, :], (SECTIONS, KVH, NBLK, KMAX)).reshape(item_count, NBLK, KMAX)
    all_grads = lax.map(head_grads, (
        split_query(queries), split_key(keys), split_key(values),
        split_query(attn_out), split_query(out_grad),
        lse.reshape(item_count, group_size, SEQ),
        starts_all, blocks_all))
    grad_q = jnp.transpose(all_grads[0].reshape(SECTIONS, KVH, SEQ, group_size * HD), (0, 2, 1, 3)).reshape(SECTIONS, SEQ, QW)
    grad_k = jnp.transpose(all_grads[1].reshape(SECTIONS, KVH, SEQ, HD), (0, 2, 1, 3)).reshape(SECTIONS, SEQ, KVW)
    grad_v = jnp.transpose(all_grads[2].reshape(SECTIONS, KVH, SEQ, HD), (0, 2, 1, 3)).reshape(SECTIONS, SEQ, KVW)
    query_grad = jnp.roll(grad_q, -1, axis=0)
    key_grad = jnp.roll(grad_k, -1, axis=0)
    value_grad = jnp.roll(grad_v, -1, axis=0)
    weight_terms = []
    for section_idx in range(SECTIONS):
        total = lax.dot_general(features[section_idx], value_grad[section_idx], (((0,), (0,)), ((), ())), preferred_element_type=jnp.float32)
        weight_terms.append(total * (SEQ ** -0.5))
    return query_grad, key_grad, value_grad, jnp.stack(weight_terms)
```

```python
import functools

import jax
import jax.numpy as jnp
from jax import lax
from jax.experimental import pallas as pl
from jax.experimental.pallas import tpu as pltpu
from jax.sharding import PartitionSpec as P

QH = 64
KVH = 8
HD = 128
GROUP = QH // KVH
LOG2E = 1.4426950408889634
KT = 256
BQ = 256
ROWS = GROUP * BQ
WIDTH = GROUP * HD
MESH = pl.DeviceIdType.MESH


def attn_kernel(own, resume, final, slots, tok, *refs):
    refs = list(refs)
    bounds = refs.pop(0)
    q_ref, do_ref, lse_ref, delta_ref, beg_ref = (refs.pop(0) for _ in range(5))
    if own:
        k_ref, v_ref = refs.pop(0), refs.pop(0)
    else:
        kv_refs = [refs.pop(0) for _ in range(slots)]
    dq_in = refs.pop(0) if resume else None
    if final == "alias":
        refs.pop(0)
    dq_ref = refs.pop(0)
    grads = [(refs.pop(0), refs.pop(0)) for _ in range(slots)]
    dkacc, dvacc, qs, dos, dqacc = (refs.pop(0) for _ in range(5))
    if not own:
        k_ref, v_ref = refs.pop(0), refs.pop(0)

    step = pl.program_id(0)
    scale = HD ** -0.5
    base = 0 if own else slots * tok
    row0 = base + step * BQ

    @pl.when(step == 0)
    def _():
        if not own:
            for slot, ref in enumerate(kv_refs):
                k_ref[slot * tok:(slot + 1) * tok, :] = ref[:, :HD]
                v_ref[slot * tok:(slot + 1) * tok, :] = ref[:, HD:]
        dkacc[...] = jnp.zeros_like(dkacc)
        dvacc[...] = jnp.zeros_like(dvacc)

    for h in range(GROUP):
        qs[h * BQ:(h + 1) * BQ, :] = q_ref[:, h * HD:(h + 1) * HD]
        dos[h * BQ:(h + 1) * BQ, :] = do_ref[:, h * HD:(h + 1) * HD]
    dqacc[...] = dq_in[0] if resume else jnp.zeros_like(dqacc)

    def tile(pair, masked):
        start = pl.multiple_of(pair * KT, KT)
        k = k_ref[pl.ds(start, KT), :]
        kt = k.T
        v = v_ref[pl.ds(start, KT), :]
        q = qs[...]
        g = dos[...]
        s = lax.dot_general(k, q, (((1,), (1,)), ((), ())), preferred_element_type=jnp.float32)
        p = jnp.exp2(s * (scale * LOG2E) - lse_ref[0, 0])
        if masked:
            u = lax.broadcasted_iota(jnp.int32, (KT, ROWS), 0) + start
            allowed = u >= beg_ref[0]
            if own:
                t = (lax.broadcasted_iota(jnp.int32, (1, ROWS), 1) & (BQ - 1)) + row0
                allowed &= u <= t
            p = jnp.where(allowed, p, 0.0)
        dp = lax.dot_general(v, g, (((1,), (1,)), ((), ())), preferred_element_type=jnp.float32)
        ds = (p * (dp - delta_ref[0, 0])).astype(jnp.bfloat16)
        pb = p.astype(jnp.bfloat16)
        dvacc[pl.ds(start, KT), :] += jnp.dot(pb, g, preferred_element_type=jnp.float32)
        dkacc[pl.ds(start, KT), :] += jnp.dot(ds, q, preferred_element_type=jnp.float32)
        dqacc[...] += jnp.dot(kt, ds, preferred_element_type=jnp.float32)

    lo = bounds[0, step]
    mid = bounds[1, step]
    last = bounds[2, step]
    edge = mid - lo

    def masked_step(i, carry):
        tile(jnp.where(i < edge, lo + i, last), True)
        return carry

    def plain_step(i, carry):
        tile(i, False)
        return carry

    lax.fori_loop(0, edge + 1 if own else edge, masked_step, 0)
    lax.fori_loop(mid, last, plain_step, 0)

    if final:
        for h in range(GROUP):
            dq_ref[0, :, h * HD:(h + 1) * HD] = (dqacc[:, h * BQ:(h + 1) * BQ].T * scale).astype(jnp.bfloat16)
    else:
        dq_ref[0] = dqacc[...]

    @pl.when(step == pl.num_programs(0) - 1)
    def _():
        for slot, (dv_ref, dk_ref) in enumerate(grads):
            at = slice(slot * tok, (slot + 1) * tok)
            dk_ref[...] = (dkacc[at, :] * scale).astype(jnp.bfloat16)
            dv_ref[...] = dvacc[at, :].astype(jnp.bfloat16)


def attention(head, own, bounds, q, do, lse, delta, beg, kv, dq_in, dq_whole, final):
    tok, width = q.shape
    blocks = tok // BQ
    slots = 1 if own else 2
    spec_q = pl.BlockSpec((BQ, WIDTH), lambda i, *_: (i, head))
    spec_row = pl.BlockSpec((1, 1, 1, ROWS), lambda i, *_: (head, i, 0, 0))
    spec_acc = pl.BlockSpec((1, HD, ROWS), lambda i, *_: (i, 0, 0))
    spec_grad = pl.BlockSpec((tok, HD), lambda i, *_: (0, 0))
    in_specs = [spec_q, spec_q, spec_row, spec_row, pl.BlockSpec((1, 1, ROWS), lambda i, *_: (i, 0, 0))]
    args = [q, do, lse, delta, beg]
    if own:
        in_specs += [pl.BlockSpec((tok, HD), lambda i, *_: (0, head))] * 2
    else:
        in_specs += [pl.BlockSpec((tok, 2 * HD), lambda i, *_: (0, 0))] * 2
    args += list(kv)
    aliases = {}
    if dq_in is not None:
        in_specs.append(spec_acc)
        args.append(dq_in)
    if final and dq_whole is not None:
        final = "alias"
        aliases = {len(args) + 1: 0}
        in_specs.append(pl.BlockSpec(memory_space=pl.ANY))
        args.append(dq_whole)
    if final:
        dq_shape = jax.ShapeDtypeStruct((1, tok, width), jnp.bfloat16)
        dq_spec = pl.BlockSpec((1, BQ, WIDTH), lambda i, *_: (0, i, head))
    else:
        dq_shape, dq_spec = jax.ShapeDtypeStruct((blocks, HD, ROWS), jnp.float32), spec_acc
    scratch = [
        pltpu.VMEM((slots * tok, HD), jnp.float32),
        pltpu.VMEM((slots * tok, HD), jnp.float32),
        pltpu.VMEM((ROWS, HD), jnp.bfloat16),
        pltpu.VMEM((ROWS, HD), jnp.bfloat16),
        pltpu.VMEM((HD, ROWS), jnp.float32),
    ]
    if not own:
        scratch += [pltpu.VMEM((slots * tok, HD), jnp.bfloat16)] * 2
    pairs = 10 if own else 22
    out = pl.pallas_call(
        functools.partial(attn_kernel, own, dq_in is not None, final, slots, tok),
        out_shape=[dq_shape] + [jax.ShapeDtypeStruct((tok, HD), jnp.bfloat16)] * (2 * slots),
        grid_spec=pltpu.PrefetchScalarGridSpec(
            num_scalar_prefetch=1,
            grid=(blocks,),
            in_specs=in_specs,
            out_specs=[dq_spec] + [spec_grad] * (2 * slots),
            scratch_shapes=scratch,
        ),
        input_output_aliases=aliases,
        compiler_params=pltpu.CompilerParams(
            dimension_semantics=("arbitrary",), vmem_limit_bytes=54 << 20),
        cost_estimate=pl.CostEstimate(
            flops=pairs * 10 * KT * ROWS * HD, transcendentals=pairs * KT * ROWS,
            bytes_accessed=10 << 20),
        name="attn_own" if own else "attn_far",
    )(bounds, *args)
    dq, rest = out[0], out[1:]
    return dq, [(rest[2 * i], rest[2 * i + 1]) for i in range(slots)]


def block_tables(starts, shard, tok):
    blocks = tok // BQ
    pos = shard * tok + jnp.arange(tok, dtype=jnp.int32)
    begin = jnp.max(jnp.where(starts[None, :] <= pos[:, None], starts[None, :], 0), axis=1)
    begin = (begin - (shard - 2) * tok).reshape(blocks, BQ)
    edge = 2 * tok // KT
    last = edge + jnp.arange(blocks, dtype=jnp.int32) * BQ // KT
    lo = begin[:, 0] // KT
    mid = jnp.minimum((begin[:, -1] + KT - 1) // KT, last)
    far = jnp.stack([jnp.minimum(lo, edge), jnp.minimum(mid, edge), jnp.full_like(lo, edge)])
    near = jnp.stack([jnp.maximum(lo, edge), jnp.maximum(mid, edge), last]) - edge
    beg = jnp.tile(begin, (1, GROUP)).reshape(blocks, 1, ROWS)
    return far.astype(jnp.int32), near.astype(jnp.int32), beg, beg - 2 * tok


def rows_kernel(do_ref, o_ref, lse_ref, delta_ref, lse2_ref):
    ones = jnp.ones((8, HD), jnp.bfloat16)
    for head in range(lse2_ref.shape[0]):
        for h in range(GROUP):
            n = head * GROUP + h
            at = slice(n * HD, (n + 1) * HD)
            prod = do_ref[:, at].astype(jnp.float32) * o_ref[:, at].astype(jnp.float32)
            high = prod.astype(jnp.bfloat16)
            low = (prod - high.astype(jnp.float32)).astype(jnp.bfloat16)
            total = lax.dot_general(ones, high, (((1,), (1,)), ((), ())), preferred_element_type=jnp.float32)
            total += lax.dot_general(ones, low, (((1,), (1,)), ((), ())), preferred_element_type=jnp.float32)
            to = slice(h * BQ, (h + 1) * BQ)
            delta_ref[head, 0, :, to] = total[:1]
            lse2_ref[head, 0, :, to] = lse_ref[n:n + 1, :] * LOG2E


def row_tables(do, o, lse):
    tok, width = do.shape
    heads = lse.shape[0]
    kv_local = heads // GROUP
    blocks = tok // BQ
    spec = pl.BlockSpec((BQ, width), lambda i: (i, 0))
    spec_row = pl.BlockSpec((kv_local, 1, 1, ROWS), lambda i: (0, i, 0, 0))
    return pl.pallas_call(
        rows_kernel,
        out_shape=[jax.ShapeDtypeStruct((kv_local, blocks, 1, ROWS), jnp.float32)] * 2,
        grid=(blocks,),
        in_specs=[spec, spec, pl.BlockSpec((heads, BQ), lambda i: (0, i))],
        out_specs=[spec_row, spec_row],
        compiler_params=pltpu.CompilerParams(
            dimension_semantics=("arbitrary",), vmem_limit_bytes=58 << 20),
        cost_estimate=pl.CostEstimate(
            flops=4 * tok * width, transcendentals=0, bytes_accessed=4 * tok * width),
        name="row_tables",
    )(do, o, lse)


def ctx_send(array, by):
    n = lax.axis_size("ctx")
    return lax.ppermute(array, "ctx", [(i, i + by) for i in range(n) if 0 <= i + by < n])


def home(array, by):
    n = lax.axis_size("ctx")
    m = lax.axis_size("section")
    pairs = [(s * n + i, (s - 1) % m * n + i - by)
             for s in range(m) for i in range(n) if i - by >= 0]
    return lax.ppermute(array, ("section", "ctx"), pairs)


def weight_kernel(nd, nc, ns, scale, *refs):
    kv_local = (len(refs) - 19) // 5
    dv_refs, dk_refs, refs = refs[:3 * kv_local], refs[3 * kv_local:4 * kv_local], refs[4 * kv_local:]
    dq_hbm, feat_hbm, out_ref, grad_ref, dq_out = refs[:5]
    dk_outs, refs = refs[5:5 + kv_local], refs[5 + kv_local:]
    (landed, dvall, feat, send, recv, fsem, hsend, hrecv, asend, arecv, rsend, rrecv, qsend, qrecv) = refs
    z = lax.axis_index("dp")
    c = lax.axis_index("ctx")
    s = lax.axis_index("section")
    cols = kv_local * HD
    rows = out_ref.shape[0]
    load = pltpu.make_async_copy(feat_hbm, feat, fsem)
    load.start()

    barrier = pltpu.get_barrier_semaphore()
    for j in range(1, nc):
        pl.semaphore_signal(barrier, inc=1, device_id={"ctx": lax.rem(c + j, nc)}, device_id_type=MESH)
    before = lax.rem(s + ns - 1, ns)
    pl.semaphore_signal(barrier, inc=1, device_id={"section": before}, device_id_type=MESH)
    has_up = z + 1 < nd
    has_down = z >= 1

    @pl.when(has_up)
    def _():
        pl.semaphore_signal(barrier, inc=1, device_id={"dp": z + 1}, device_id_type=MESH)

    @pl.when(has_down)
    def _():
        pl.semaphore_signal(barrier, inc=1, device_id={"dp": z - 1}, device_id_type=MESH)

    pl.semaphore_wait(barrier, nc + jnp.where(has_up, 1, 0) + jnp.where(has_down, 1, 0))

    def hop(src, way, k):
        return pltpu.make_async_remote_copy(
            src_ref=dvall.at[src], dst_ref=dvall.at[src],
            send_sem=asend.at[way, k], recv_sem=arecv.at[src],
            device_id={"dp": z + 1 if way == 0 else z - 1}, device_id_type=MESH)

    def each_hop(k, act):
        up, down = z - k, z + k

        @pl.when((up >= 0) & has_up)
        def _():
            act(hop(up, 0, k))

        @pl.when((down < nd) & has_down)
        def _():
            act(hop(down, 1, k))

    def share(j, src, target):
        return pltpu.make_async_remote_copy(
            src_ref=send.at[j - 1, src], dst_ref=recv.at[j - 1, src],
            send_sem=rsend.at[j - 1, src], recv_sem=rrecv.at[j - 1, src],
            device_id={"ctx": target}, device_id_type=MESH)

    def product(target, src):
        return lax.dot_general(
            feat[:, pl.ds(pl.multiple_of(target * rows, 128), rows)], dvall[src],
            (((0,), (0,)), ((), ())), preferred_element_type=jnp.float32)

    def process(src):
        def one(j, carry):
            target = lax.rem(c + j, nc)
            send[j - 1, src] = product(target, src).astype(jnp.bfloat16)
            share(j, src, target).start()
            return carry

        lax.fori_loop(1, nc, one, 0)
        out_ref[:, pl.ds(pl.multiple_of(src * cols, 128), cols)] = product(c, src)

    homes = [
        pltpu.make_async_remote_copy(
            src_ref=dv_refs[3 * head], dst_ref=landed.at[head],
            send_sem=hsend.at[head], recv_sem=hrecv.at[head],
            device_id={"section": before}, device_id_type=MESH)
        for head in range(kv_local)]
    later = [
        pltpu.make_async_remote_copy(
            src_ref=src, dst_ref=dst, send_sem=qsend.at[i], recv_sem=qrecv.at[i],
            device_id={"section": before}, device_id_type=MESH)
        for i, (src, dst) in enumerate(zip([dq_hbm, *dk_refs], [dq_out, *dk_outs]))]
    for copy in homes + later:
        copy.start()
    for head, copy in enumerate(homes):
        at = slice(head * HD, (head + 1) * HD)
        copy.wait_recv()
        total = landed[head].astype(jnp.float32) + dv_refs[3 * head + 1][...] + dv_refs[3 * head + 2][...]
        dvall[z, :, at] = total.astype(jnp.bfloat16)
    each_hop(0, lambda copy: copy.start())
    grad_ref[...] = dvall[z]
    load.wait()
    process(z)
    for k in range(1, nd):
        up, down = z - k, z + k

        @pl.when(up >= 0)
        def _():
            hop(up, 0, 0).wait_recv()

        @pl.when(down < nd)
        def _():
            hop(down, 1, 0).wait_recv()

        if k < nd - 1:
            each_hop(k, lambda copy: copy.start())

        @pl.when(up >= 0)
        def _():
            process(up)

        @pl.when(down < nd)
        def _():
            process(down)

    for copy in homes:
        copy.wait_send()
    for copy in later:
        copy.wait()
    for k in range(nd - 1):
        each_hop(k, lambda copy: copy.wait_send())
    for src in range(nd):
        at = slice(src * cols, (src + 1) * cols)
        total = out_ref[:, at]
        for j in range(1, nc):
            share(j, src, c).wait_recv()
            total = total + recv[j - 1, src]
        out_ref[:, at] = total * scale

    def drain(i, carry):
        share(i // nd + 1, i % nd, c).wait_send()
        return carry

    lax.fori_loop(0, (nc - 1) * nd, drain, 0)


def weight_grad(feat, dq, dv_parts, dk_own, nd, nc, ns, scale):
    tok, width = feat.shape
    rows = width // nc
    kv_local = len(dv_parts)
    cols = kv_local * HD
    return pl.pallas_call(
        functools.partial(weight_kernel, nd, nc, ns, scale),
        out_shape=[jax.ShapeDtypeStruct((rows, nd * cols), jnp.float32),
                   jax.ShapeDtypeStruct((tok, cols), jnp.bfloat16),
                   jax.ShapeDtypeStruct(dq.shape, dq.dtype)]
        + [jax.ShapeDtypeStruct((tok, HD), jnp.bfloat16)] * kv_local,
        in_specs=[pl.BlockSpec(memory_space=pltpu.VMEM)] * (4 * kv_local) + [pl.BlockSpec(memory_space=pl.ANY)] * 2,
        out_specs=[pl.BlockSpec(memory_space=pltpu.VMEM)] * 2 + [pl.BlockSpec(memory_space=pl.ANY)]
        + [pl.BlockSpec(memory_space=pltpu.VMEM)] * kv_local,
        scratch_shapes=[
            pltpu.VMEM((kv_local, tok, HD), jnp.bfloat16),
            pltpu.VMEM((nd, tok, cols), jnp.bfloat16),
            pltpu.VMEM((tok, width), jnp.bfloat16),
            pltpu.VMEM((nc - 1, nd, rows, cols), jnp.bfloat16),
            pltpu.VMEM((nc - 1, nd, rows, cols), jnp.bfloat16),
            pltpu.SemaphoreType.DMA,
            pltpu.SemaphoreType.DMA((kv_local,)),
            pltpu.SemaphoreType.DMA((kv_local,)),
            pltpu.SemaphoreType.DMA((2, nd)),
            pltpu.SemaphoreType.DMA((nd,)),
            pltpu.SemaphoreType.DMA((nc - 1, nd)),
            pltpu.SemaphoreType.DMA((nc - 1, nd)),
            pltpu.SemaphoreType.DMA((kv_local + 1,)),
            pltpu.SemaphoreType.DMA((kv_local + 1,)),
        ],
        compiler_params=pltpu.CompilerParams(
            collective_id=0, has_side_effects=True, vmem_limit_bytes=58 << 20),
        cost_estimate=pl.CostEstimate(
            flops=2 * tok * width * nd * cols, transcendentals=0, bytes_accessed=8 << 20),
        name="weight_grad",
    )(*[part for parts in dv_parts for part in parts], *dk_own, dq, feat)


def weight_plain(feat, dv, nd, nc, scale):
    shard = lax.axis_index("ctx")
    rows = feat.shape[1] // nc
    dv_all = lax.all_gather(dv, "dp", axis=1, tiled=True)

    def partial(target):
        cols = lax.dynamic_slice_in_dim(feat, target * rows, rows, 1)
        return lax.dot_general(cols, dv_all, (((0,), (0,)), ((), ())),
                               preferred_element_type=jnp.float32)

    total = partial(shard)
    for by in range(1, nc):
        sent = partial((shard + by) % nc).astype(jnp.bfloat16)
        total = total + lax.ppermute(sent, "ctx", [(i, (i + by) % nc) for i in range(nc)])
    return total * scale


def local(features, queries, keys, values, attn_out, out_grad, lse, doc_starts, key_blocks):
    tok = queries.shape[1]
    kv_local = keys.shape[2] // HD
    shard = lax.axis_index("ctx")
    nc = lax.axis_size("ctx")
    nd = lax.axis_size("dp")
    ns = lax.axis_size("section")
    q, do, k, v = queries[0], out_grad[0], keys[0], values[0]
    windows = []
    for head in range(kv_local):
        at = slice(head * HD, (head + 1) * HD)
        kv = jnp.concatenate([k[:, at], v[:, at]], axis=1)
        windows.append((ctx_send(kv, 2), ctx_send(kv, 1)))
    far, near, beg_far, beg_near = block_tables(doc_starts[0], shard, tok)
    delta, lse2 = row_tables(do, attn_out[0], lse[0])
    dq_whole = None
    dk_parts, dv_parts = [], []
    back = ()
    for head in range(kv_local):
        def near_part(dq, final, bounds):
            return attention(head, True, bounds, q, do, lse2, delta, beg_near, (k, v), dq, dq_whole, final)

        def far_part(dq, final, bounds):
            return attention(head, False, bounds, q, do, lse2, delta, beg_far, windows[head], dq, dq_whole, final)

        if head < kv_local - 1:
            dq, ((dv2, dk2),) = near_part(None, False, near)
            dq, ((dv0, dk0), (dv1, dk1)) = far_part(dq, True, far)
            far, _ = lax.optimization_barrier((far, dv0))
        else:
            dq, ((dv0, dk0), (dv1, dk1)) = far_part(None, False, far)
            near, _ = lax.optimization_barrier((near, back))
            dq, ((dv2, dk2),) = near_part(dq, True, near)
        dq_whole = dq
        back = (home(dv0, 2), home(dv1, 1), home(dk0, 2), home(dk1, 1))
        dv_parts.append((dv2, *back[:2]))
        dk_parts.append((dk2, *back[2:]))

    def gather(parts):
        return jnp.concatenate(
            [own.astype(jnp.float32) + two + one for own, two, one in parts], axis=1).astype(jnp.bfloat16)

    scale = (tok * nc) ** -0.5
    feat = features[0]
    dk_own = [parts[0] for parts in dk_parts]
    if feat.shape[1] // nc % 128 == 0:
        weight, value_grad, query_grad, *dk_own = weight_grad(
            feat, dq_whole, dv_parts, dk_own, nd, nc, ns, scale)
    else:
        query_grad = home(dq_whole, 0)
        dk_own = [home(own, 0) for own in dk_own]
        value_grad = gather([(home(own, 0), two, one) for own, two, one in dv_parts])
        weight = weight_plain(feat, value_grad, nd, nc, scale)
    key_grad = gather([(own, *parts[1:]) for own, parts in zip(dk_own, dk_parts)])
    return query_grad, key_grad[None], value_grad[None], weight[None]


def solution(mesh):
    placed = (
        P("section", "ctx", "dp"),
        P("section", "ctx", "dp"),
        P("section", "ctx", "dp"),
        P("section", "ctx", "dp"),
        P("section", "ctx", "dp"),
        P("section", "ctx", "dp"),
        P("section", "dp", "ctx"),
        P("section", None),
        P("section", "ctx", None),
    )
    return jax.shard_map(
        local,
        mesh=mesh,
        in_specs=placed,
        out_specs=(
            P("section", "ctx", "dp"),
            P("section", "ctx", "dp"),
            P("section", "ctx", "dp"),
            P("section", ("dp", "ctx"), None),
        ),
        check_vma=False,
    )
```

```python
import functools

import jax
import jax.numpy as jnp
from jax import lax
from jax.experimental import pallas as pl
from jax.experimental.pallas import tpu as pltpu
from jax.sharding import PartitionSpec as P

QH = 64
KVH = 8
HD = 128
GROUP = QH // KVH
LOG2E = 1.4426950408889634
KT = 256
BQ = 256
ROWS = GROUP * BQ
WIDTH = GROUP * HD
MESH = pl.DeviceIdType.MESH


def attn_kernel(own, resume, final, slots, tok, *refs):
    refs = list(refs)
    bounds = refs.pop(0)
    q_ref, do_ref, lse_ref, delta_ref, beg_ref = (refs.pop(0) for _ in range(5))
    if own:
        k_ref, v_ref = refs.pop(0), refs.pop(0)
    else:
        kv_refs = [refs.pop(0) for _ in range(slots)]
    dq_in = refs.pop(0) if resume else None
    dq_ref = refs.pop(0)
    grads = [refs.pop(0) for _ in range(slots)]
    dkacc, dvacc, qs, dos, dqacc = (refs.pop(0) for _ in range(5))
    if not own:
        k_ref, v_ref = refs.pop(0), refs.pop(0)

    step = pl.program_id(0)
    scale = HD ** -0.5
    base = 0 if own else slots * tok
    row0 = base + step * BQ

    @pl.when(step == 0)
    def _():
        if not own:
            for slot, ref in enumerate(kv_refs):
                k_ref[slot * tok:(slot + 1) * tok, :] = ref[:, :HD]
                v_ref[slot * tok:(slot + 1) * tok, :] = ref[:, HD:]
        dkacc[...] = jnp.zeros_like(dkacc)
        dvacc[...] = jnp.zeros_like(dvacc)

    for h in range(GROUP):
        qs[h * BQ:(h + 1) * BQ, :] = q_ref[:, h * HD:(h + 1) * HD]
        dos[h * BQ:(h + 1) * BQ, :] = do_ref[:, h * HD:(h + 1) * HD]
    dqacc[...] = dq_in[0] if resume else jnp.zeros_like(dqacc)

    def tile(pair, masked):
        start = pl.multiple_of(pair * KT, KT)
        k = k_ref[pl.ds(start, KT), :]
        kt = k.T
        v = v_ref[pl.ds(start, KT), :]
        q = qs[...]
        g = dos[...]
        s = lax.dot_general(k, q, (((1,), (1,)), ((), ())), preferred_element_type=jnp.float32)
        p = jnp.exp2(s * (scale * LOG2E) - lse_ref[0, 0])
        if masked:
            u = lax.broadcasted_iota(jnp.int32, (KT, ROWS), 0) + start
            allowed = u >= beg_ref[0]
            if own:
                t = (lax.broadcasted_iota(jnp.int32, (1, ROWS), 1) & (BQ - 1)) + row0
                allowed &= u <= t
            p = jnp.where(allowed, p, 0.0)
        dp = lax.dot_general(v, g, (((1,), (1,)), ((), ())), preferred_element_type=jnp.float32)
        ds = (p * (dp - delta_ref[0, 0])).astype(jnp.bfloat16)
        pb = p.astype(jnp.bfloat16)
        dvacc[pl.ds(start, KT), :] += jnp.dot(pb, g, preferred_element_type=jnp.float32)
        dkacc[pl.ds(start, KT), :] += jnp.dot(ds, q, preferred_element_type=jnp.float32)
        dqacc[...] += jnp.dot(kt, ds, preferred_element_type=jnp.float32)

    lo = bounds[0, step]
    mid = bounds[1, step]
    last = bounds[2, step]
    edge = mid - lo

    def masked_step(i, carry):
        tile(jnp.where(i < edge, lo + i, last), True)
        return carry

    def plain_step(i, carry):
        tile(i, False)
        return carry

    lax.fori_loop(0, edge + 1 if own else edge, masked_step, 0)
    lax.fori_loop(mid, last, plain_step, 0)

    if final:
        for h in range(GROUP):
            dq_ref[0, :, h * HD:(h + 1) * HD] = (dqacc[:, h * BQ:(h + 1) * BQ].T * scale).astype(jnp.bfloat16)
    else:
        dq_ref[0] = dqacc[...]

    @pl.when(step == pl.num_programs(0) - 1)
    def _():
        for slot, ref in enumerate(grads):
            at = slice(slot * tok, (slot + 1) * tok)
            ref[0] = dvacc[at, :].astype(jnp.bfloat16)
            ref[1] = (dkacc[at, :] * scale).astype(jnp.bfloat16)


def attention(head, own, bounds, q, do, lse, delta, beg, kv, dq_in, final):
    tok, width = q.shape
    blocks = tok // BQ
    slots = 1 if own else 2
    spec_q = pl.BlockSpec((BQ, WIDTH), lambda i, *_: (i, head))
    spec_row = pl.BlockSpec((1, 1, 1, ROWS), lambda i, *_: (head, i, 0, 0))
    spec_acc = pl.BlockSpec((1, HD, ROWS), lambda i, *_: (i, 0, 0))
    spec_grad = pl.BlockSpec((2, tok, HD), lambda i, *_: (0, 0, 0))
    in_specs = [spec_q, spec_q, spec_row, spec_row, pl.BlockSpec((1, 1, ROWS), lambda i, *_: (i, 0, 0))]
    args = [q, do, lse, delta, beg]
    if own:
        in_specs += [pl.BlockSpec((tok, HD), lambda i, *_: (0, head))] * 2
    else:
        in_specs += [pl.BlockSpec((tok, 2 * HD), lambda i, *_: (0, 0))] * 2
    args += list(kv)
    if dq_in is not None:
        in_specs.append(spec_acc)
        args.append(dq_in)
    if final:
        dq_shape = jax.ShapeDtypeStruct((1, tok, WIDTH), jnp.bfloat16)
        dq_spec = pl.BlockSpec((1, BQ, WIDTH), lambda i, *_: (0, i, 0))
    else:
        dq_shape, dq_spec = jax.ShapeDtypeStruct((blocks, HD, ROWS), jnp.float32), spec_acc
    scratch = [
        pltpu.VMEM((slots * tok, HD), jnp.float32),
        pltpu.VMEM((slots * tok, HD), jnp.float32),
        pltpu.VMEM((ROWS, HD), jnp.bfloat16),
        pltpu.VMEM((ROWS, HD), jnp.bfloat16),
        pltpu.VMEM((HD, ROWS), jnp.float32),
    ]
    if not own:
        scratch += [pltpu.VMEM((slots * tok, HD), jnp.bfloat16)] * 2
    pairs = 10 if own else 22
    out = pl.pallas_call(
        functools.partial(attn_kernel, own, dq_in is not None, final, slots, tok),
        out_shape=[dq_shape] + [jax.ShapeDtypeStruct((2, tok, HD), jnp.bfloat16)] * slots,
        grid_spec=pltpu.PrefetchScalarGridSpec(
            num_scalar_prefetch=1,
            grid=(blocks,),
            in_specs=in_specs,
            out_specs=[dq_spec] + [spec_grad] * slots,
            scratch_shapes=scratch,
        ),
        compiler_params=pltpu.CompilerParams(
            dimension_semantics=("arbitrary",), vmem_limit_bytes=54 << 20),
        cost_estimate=pl.CostEstimate(
            flops=pairs * 10 * KT * ROWS * HD, transcendentals=pairs * KT * ROWS,
            bytes_accessed=10 << 20),
        name="attn_own" if own else "attn_far",
    )(bounds, *args)
    return out[0], list(out[1:])


def block_tables(starts, shard, tok):
    blocks = tok // BQ
    pos = shard * tok + jnp.arange(tok, dtype=jnp.int32)
    begin = jnp.max(jnp.where(starts[None, :] <= pos[:, None], starts[None, :], 0), axis=1)
    begin = (begin - (shard - 2) * tok).reshape(blocks, BQ)
    edge = 2 * tok // KT
    last = edge + jnp.arange(blocks, dtype=jnp.int32) * BQ // KT
    lo = begin[:, 0] // KT
    mid = jnp.minimum((begin[:, -1] + KT - 1) // KT, last)
    far = jnp.stack([jnp.minimum(lo, edge), jnp.minimum(mid, edge), jnp.full_like(lo, edge)])
    near = jnp.stack([jnp.maximum(lo, edge), jnp.maximum(mid, edge), last]) - edge
    beg = jnp.tile(begin, (1, GROUP)).reshape(blocks, 1, ROWS)
    return far.astype(jnp.int32), near.astype(jnp.int32), beg, beg - 2 * tok


def rows_kernel(do_ref, o_ref, lse_ref, delta_ref, lse2_ref):
    ones = jnp.ones((8, 2 * HD), jnp.bfloat16)
    for head in range(lse2_ref.shape[0]):
        for h in range(GROUP):
            n = head * GROUP + h
            at = slice(n * HD, (n + 1) * HD)
            prod = do_ref[:, at].astype(jnp.float32) * o_ref[:, at].astype(jnp.float32)
            high = prod.astype(jnp.bfloat16)
            low = (prod - high.astype(jnp.float32)).astype(jnp.bfloat16)
            total = lax.dot_general(ones, jnp.concatenate([high, low], axis=1), (((1,), (1,)), ((), ())),
                                    preferred_element_type=jnp.float32)
            to = slice(h * BQ, (h + 1) * BQ)
            delta_ref[head, 0, :, to] = total[:1]
            lse2_ref[head, 0, :, to] = lse_ref[n:n + 1, :] * LOG2E


def row_tables(do, o, lse):
    tok, width = do.shape
    heads = lse.shape[0]
    kv_local = heads // GROUP
    blocks = tok // BQ
    spec = pl.BlockSpec((BQ, width), lambda i: (i, 0))
    spec_row = pl.BlockSpec((kv_local, 1, 1, ROWS), lambda i: (0, i, 0, 0))
    return pl.pallas_call(
        rows_kernel,
        out_shape=[jax.ShapeDtypeStruct((kv_local, blocks, 1, ROWS), jnp.float32)] * 2,
        grid=(blocks,),
        in_specs=[spec, spec, pl.BlockSpec((heads, BQ), lambda i: (0, i))],
        out_specs=[spec_row, spec_row],
        compiler_params=pltpu.CompilerParams(
            dimension_semantics=("arbitrary",), vmem_limit_bytes=58 << 20),
        cost_estimate=pl.CostEstimate(
            flops=4 * tok * width, transcendentals=0, bytes_accessed=4 * tok * width),
        name="row_tables",
    )(do, o, lse)


def ctx_send(array, by):
    n = lax.axis_size("ctx")
    return lax.ppermute(array, "ctx", [(i, i + by) for i in range(n) if 0 <= i + by < n])


def home(array, by):
    n = lax.axis_size("ctx")
    m = lax.axis_size("section")
    pairs = [(s * n + i, (s - 1) % m * n + i - by)
             for s in range(m) for i in range(n) if i - by >= 0]
    return lax.ppermute(array, ("section", "ctx"), pairs)


def tail_kernel(nd, nc, ns, wscale, kv_local, *refs):
    refs = list(refs)
    take = lambda n: [refs.pop(0) for _ in range(n)]
    last = kv_local - 1
    before_parts = [take(3) for _ in range(last)]
    (far2, far1, lse_ref, delta_ref, beg_ref, k_ref, v_ref, q_hbm, do_hbm, dq_hbm, feat_hbm,
     w_ref, vg_ref, kg_ref, dq_ref,
     feat, qv, gv, dqv, qs, dos, dqs, dkacc, dvacc, own, landed, back, dvall, dts, send, recv, acc,
     lsem, osend, orecv, bsend, brecv, asend, arecv, rsend, rrecv, qsend, qrecv) = refs
    z = lax.axis_index("dp")
    c = lax.axis_index("ctx")
    s = lax.axis_index("section")
    scale = HD ** -0.5
    tok = k_ref.shape[0]
    rows = w_ref.shape[0]
    steps = tok // BQ
    cols = slice(last * HD, (last + 1) * HD)
    wide = pl.ds(last * WIDTH, WIDTH)

    loads = [
        pltpu.make_async_copy(src, dst, lsem.at[i])
        for i, (src, dst) in enumerate((
            (q_hbm.at[:, wide], qv), (do_hbm.at[:, wide], gv), (dq_hbm, dqv), (feat_hbm, feat)))]
    for copy in loads:
        copy.start()

    has_up = z + 1 < nd
    has_down = z >= 1
    to = lax.rem(s + ns - 1, ns)
    come = lax.rem(s + 1, ns)
    barrier = pltpu.get_barrier_semaphore()

    def greet(**device):
        pl.semaphore_signal(barrier, inc=1, device_id=device, device_id_type=MESH)

    for j in range(1, nc):
        greet(ctx=lax.rem(c + j, nc))
    greet(section=come)
    for by in (1, 2):
        @pl.when(c + by < nc)
        def _():
            greet(section=come, ctx=c + by)

    @pl.when(has_up)
    def _():
        greet(dp=z + 1)

    @pl.when(has_down)
    def _():
        greet(dp=z - 1)

    one = lambda cond: jnp.where(cond, 1, 0)
    pl.semaphore_wait(barrier, nc + one(c >= 1) + one(c >= 2) + one(has_up) + one(has_down))

    def hand(src, head, kind):
        return pltpu.make_async_remote_copy(
            src_ref=src.at[kind], dst_ref=landed.at[head, kind],
            send_sem=osend.at[head, kind], recv_sem=orecv.at[head, kind],
            device_id={"section": to}, device_id_type=MESH)

    def partial_home(src, by, kind):
        return pltpu.make_async_remote_copy(
            src_ref=src.at[kind], dst_ref=back.at[by - 1, kind],
            send_sem=bsend.at[by - 1, kind], recv_sem=brecv.at[by - 1, kind],
            device_id={"section": to, "ctx": c - by}, device_id_type=MESH)

    for head in range(last):
        hand(before_parts[head][0], head, 0).start()
    for kind in (0, 1):
        for by, src in ((2, far2), (1, far1)):
            @pl.when(c >= by)
            def _():
                partial_home(src, by, kind).start()

            @pl.when(c + by >= nc)
            def _():
                back[by - 1, kind] = jnp.zeros((tok, HD), jnp.bfloat16)
    for head in range(last):
        hand(before_parts[head][0], head, 1).start()

    def hop(head, src, way, k):
        return pltpu.make_async_remote_copy(
            src_ref=dvall.at[head, src], dst_ref=dvall.at[head, src],
            send_sem=asend.at[head, way, k], recv_sem=arecv.at[head, src],
            device_id={"dp": z + 1 if way == 0 else z - 1}, device_id_type=MESH)

    def each_hop(head, k, act):
        up, down = z - k, z + k

        @pl.when((up >= 0) & has_up)
        def _():
            act(hop(head, up, 0, k))

        @pl.when((down < nd) & has_down)
        def _():
            act(hop(head, down, 1, k))

    def share(j, head, src, target):
        return pltpu.make_async_remote_copy(
            src_ref=send.at[j - 1, head, src], dst_ref=recv.at[j - 1, head, src],
            send_sem=rsend.at[j - 1, head, src], recv_sem=rrecv.at[j - 1, head, src],
            device_id={"ctx": target}, device_id_type=MESH)

    def product(target):
        return jnp.dot(dts[...], feat[:, pl.ds(pl.multiple_of(target * rows, 128), rows)],
                       preferred_element_type=jnp.float32)

    def process(head, src):
        dts[...] = dvall[head, src].T

        def send_one(j, carry):
            target = lax.rem(c + j, nc)
            send[j - 1, head, src] = product(target).astype(jnp.bfloat16)
            share(j, head, src, target).start()
            return carry

        lax.fori_loop(1, nc, send_one, 0)
        acc[head, src] = product(c)

    def advance(head, k):
        up, down = z - k, z + k

        @pl.when(up >= 0)
        def _():
            hop(head, up, 0, 0).wait_recv()

        @pl.when(down < nd)
        def _():
            hop(head, down, 1, 0).wait_recv()

        if k < nd - 1:
            each_hop(head, k, lambda copy: copy.start())

        @pl.when(up >= 0)
        def _():
            process(head, up)

        @pl.when(down < nd)
        def _():
            process(head, down)

    def begin(head, two, one):
        at = slice(head * HD, (head + 1) * HD)
        total = (landed[head, 0].astype(jnp.float32) + two[0] + one[0]).astype(jnp.bfloat16)
        dvall[head, z] = total
        each_hop(head, 0, lambda copy: copy.start())
        vg_ref[:, at] = total

    def send_dq(i):
        at = pl.ds(i * BQ, BQ)
        return pltpu.make_async_remote_copy(
            src_ref=dqs.at[at], dst_ref=dq_ref.at[at], send_sem=qsend.at[i], recv_sem=qrecv.at[i],
            device_id={"section": to}, device_id_type=MESH)

    def attend(i):
        for h in range(GROUP):
            qs[h * BQ:(h + 1) * BQ, :] = qv[i * BQ:(i + 1) * BQ, h * HD:(h + 1) * HD]
            dos[h * BQ:(h + 1) * BQ, :] = gv[i * BQ:(i + 1) * BQ, h * HD:(h + 1) * HD]

        def tile(pair, carry):
            start = pl.multiple_of(pair * KT, KT)
            k = k_ref[pl.ds(start, KT), cols]
            kt = k.T
            v = v_ref[pl.ds(start, KT), cols]
            q = qs[...]
            g = dos[...]
            sc = lax.dot_general(k, q, (((1,), (1,)), ((), ())), preferred_element_type=jnp.float32)
            p = jnp.exp2(sc * (scale * LOG2E) - lse_ref[last, i])
            u = lax.broadcasted_iota(jnp.int32, (KT, ROWS), 0) + start
            t = (lax.broadcasted_iota(jnp.int32, (1, ROWS), 1) & (BQ - 1)) + i * BQ
            p = jnp.where((u >= beg_ref[i]) & (u <= t), p, 0.0)
            dp = lax.dot_general(v, g, (((1,), (1,)), ((), ())), preferred_element_type=jnp.float32)
            ds = (p * (dp - delta_ref[last, i])).astype(jnp.bfloat16)
            pb = p.astype(jnp.bfloat16)
            dvacc[pl.ds(start, KT), :] += jnp.dot(pb, g, preferred_element_type=jnp.float32)
            dkacc[pl.ds(start, KT), :] += jnp.dot(ds, q, preferred_element_type=jnp.float32)
            dqv[i] += jnp.dot(kt, ds, preferred_element_type=jnp.float32)
            return carry

        lax.fori_loop(0, i + 1, tile, 0)
        for h in range(GROUP):
            dqs[i * BQ:(i + 1) * BQ, h * HD:(h + 1) * HD] = (
                dqv[i, :, h * BQ:(h + 1) * BQ].T * scale).astype(jnp.bfloat16)
        send_dq(i).start()

    dkacc[...] = jnp.zeros_like(dkacc)
    dvacc[...] = jnp.zeros_like(dvacc)
    for copy in loads[:3]:
        copy.wait()
    for head in range(last):
        hand(before_parts[head][0], head, 0).wait_recv()
        begin(head, before_parts[head][1], before_parts[head][2])
    loads[3].wait()
    for head in range(last):
        process(head, z)
    for i in reversed(range(steps)):
        attend(i)
        k = steps - i
        if i > 0:
            for head in range(last):
                if k < nd:
                    advance(head, k)
    own[0] = dvacc[...].astype(jnp.bfloat16)
    hand(own, last, 0).start()
    own[1] = (dkacc[...] * scale).astype(jnp.bfloat16)
    hand(own, last, 1).start()
    for head in range(last):
        for k in range(steps, nd):
            advance(head, k)
    for by in (2, 1):
        @pl.when(c + by < nc)
        def _():
            partial_home(far1, by, 0).wait_recv()
    hand(own, last, 0).wait_recv()
    begin(last, back.at[1], back.at[0])
    process(last, z)
    for head in range(kv_local):
        if head == last:
            for by in (2, 1):
                @pl.when(c + by < nc)
                def _():
                    partial_home(far1, by, 1).wait_recv()
            two, one_ref = back.at[1], back.at[0]
            hand(own, head, 1).wait_recv()
        else:
            two, one_ref = before_parts[head][1:]
            hand(before_parts[head][0], head, 1).wait_recv()
        kg_ref[:, head * HD:(head + 1) * HD] = (
            landed[head, 1].astype(jnp.float32) + two[1] + one_ref[1]).astype(jnp.bfloat16)
    for k in range(1, nd):
        advance(last, k)

    for head in range(kv_local):
        for kind in (0, 1):
            hand(own if head == last else before_parts[head][0], head, kind).wait_send()
        for k in range(nd - 1):
            each_hop(head, k, lambda copy: copy.wait_send())
    for kind in (0, 1):
        for by, src in ((2, far2), (1, far1)):
            @pl.when(c >= by)
            def _():
                partial_home(src, by, kind).wait_send()
    for i in range(steps):
        send_dq(i).wait()
    for head in range(kv_local):
        for src in range(nd):
            total = acc[head, src]
            for j in range(1, nc):
                share(j, head, src, c).wait_recv()
                total = total + recv[j - 1, head, src]
            at = (src * kv_local + head) * HD
            w_ref[:, at:at + HD] = total.T * wscale

    def drain(i, carry):
        share(1 + i // (kv_local * nd), i // nd % kv_local, i % nd, c).wait_send()
        return carry

    lax.fori_loop(0, (nc - 1) * kv_local * nd, drain, 0)


def tail(feat, q, do, k, v, lse, delta, beg, parts, far, dq, nd, nc, ns, scale):
    tok, width = feat.shape
    rows = width // nc
    kv_local = len(parts) + 1
    steps = tok // BQ
    bf16, f32 = jnp.bfloat16, jnp.float32
    vmem, dma = pltpu.VMEM, pltpu.SemaphoreType.DMA
    whole = pl.BlockSpec(memory_space=pltpu.VMEM)
    return pl.pallas_call(
        functools.partial(tail_kernel, nd, nc, ns, scale, kv_local),
        out_shape=[
            jax.ShapeDtypeStruct((rows, nd * kv_local * HD), f32),
            jax.ShapeDtypeStruct((tok, kv_local * HD), bf16),
            jax.ShapeDtypeStruct((tok, kv_local * HD), bf16),
            jax.ShapeDtypeStruct((tok, WIDTH), bf16),
        ],
        in_specs=[whole] * (3 * len(parts) + 7) + [pl.BlockSpec(memory_space=pl.ANY)] * 4,
        out_specs=[whole] * 4,
        scratch_shapes=[
            vmem((tok, width), bf16),
            vmem((tok, WIDTH), bf16),
            vmem((tok, WIDTH), bf16),
            vmem((steps, HD, ROWS), f32),
            vmem((ROWS, HD), bf16),
            vmem((ROWS, HD), bf16),
            vmem((tok, WIDTH), bf16),
            vmem((tok, HD), f32),
            vmem((tok, HD), f32),
            vmem((2, tok, HD), bf16),
            vmem((kv_local, 2, tok, HD), bf16),
            vmem((2, 2, tok, HD), bf16),
            vmem((kv_local, nd, tok, HD), bf16),
            vmem((HD, tok), bf16),
            vmem((nc - 1, kv_local, nd, HD, rows), bf16),
            vmem((nc - 1, kv_local, nd, HD, rows), bf16),
            vmem((kv_local, nd, HD, rows), f32),
            dma((4,)),
            dma((kv_local, 2)),
            dma((kv_local, 2)),
            dma((2, 2)),
            dma((2, 2)),
            dma((kv_local, 2, nd)),
            dma((kv_local, nd)),
            dma((nc - 1, kv_local, nd)),
            dma((nc - 1, kv_local, nd)),
            dma((steps,)),
            dma((steps,)),
        ],
        compiler_params=pltpu.CompilerParams(
            collective_id=0, has_side_effects=True, vmem_limit_bytes=60 << 20),
        cost_estimate=pl.CostEstimate(
            flops=2 * tok * width * nd * kv_local * HD + 10 * 10 * KT * ROWS * HD,
            transcendentals=10 * KT * ROWS, bytes_accessed=20 << 20),
        name="tail",
    )(*[part for head in parts for part in head], *far, lse, delta, beg, k, v, q, do, dq, feat)


def weight_plain(feat, dv, nd, nc, scale):
    shard = lax.axis_index("ctx")
    rows = feat.shape[1] // nc
    dv_all = lax.all_gather(dv, "dp", axis=1, tiled=True)

    def partial(target):
        cols = lax.dynamic_slice_in_dim(feat, target * rows, rows, 1)
        return lax.dot_general(cols, dv_all, (((0,), (0,)), ((), ())),
                               preferred_element_type=jnp.float32)

    total = partial(shard)
    for by in range(1, nc):
        sent = partial((shard + by) % nc).astype(jnp.bfloat16)
        total = total + lax.ppermute(sent, "ctx", [(i, (i + by) % nc) for i in range(nc)])
    return total * scale


def local(features, queries, keys, values, attn_out, out_grad, lse, doc_starts, key_blocks):
    tok = queries.shape[1]
    kv_local = keys.shape[2] // HD
    shard = lax.axis_index("ctx")
    nc = lax.axis_size("ctx")
    nd = lax.axis_size("dp")
    ns = lax.axis_size("section")
    q, do, k, v = queries[0], out_grad[0], keys[0], values[0]
    windows = []
    for head in range(kv_local):
        at = slice(head * HD, (head + 1) * HD)
        kv = jnp.concatenate([k[:, at], v[:, at]], axis=1)
        windows.append((ctx_send(kv, 2), ctx_send(kv, 1)))
    far, near, beg_far, beg_near = block_tables(doc_starts[0], shard, tok)
    delta, lse2 = row_tables(do, attn_out[0], lse[0])
    scale = (tok * nc) ** -0.5
    feat = features[0]
    last = kv_local - 1
    dq_parts, parts = [], []
    for head in range(last):
        dq, (own,) = attention(head, True, near, q, do, lse2, delta, beg_near, (k, v), None, False)
        dq, (two, one) = attention(head, False, far, q, do, lse2, delta, beg_far, windows[head], dq, True)
        far, _ = lax.optimization_barrier((far, two))
        dq_parts.append(home(dq, 0))
        parts.append((own, home(two, 2), home(one, 1)))
    dq, (two, one) = attention(last, False, far, q, do, lse2, delta, beg_far, windows[last], None, False)
    if feat.shape[1] // nc % 128 == 0:
        weight, value_grad, key_grad, dq = tail(
            feat, q, do, k, v, lse2, delta, beg_near, parts, (two, one), dq, nd, nc, ns, scale)
        dq_parts.append(dq[None])
    else:
        dq, (own,) = attention(last, True, near, q, do, lse2, delta, beg_near, (k, v), dq, True)
        dq_parts.append(home(dq, 0))
        parts.append((own, home(two, 2), home(one, 1)))
        grads = [(home(own, 0).astype(jnp.float32) + two + one).astype(jnp.bfloat16) for own, two, one in parts]
        value_grad = jnp.concatenate([grad[0] for grad in grads], axis=1)
        key_grad = jnp.concatenate([grad[1] for grad in grads], axis=1)
        weight = weight_plain(feat, value_grad, nd, nc, scale)
    query_grad = jnp.concatenate(dq_parts, axis=2)
    return query_grad, key_grad[None], value_grad[None], weight[None]


def solution(mesh):
    placed = (
        P("section", "ctx", "dp"),
        P("section", "ctx", "dp"),
        P("section", "ctx", "dp"),
        P("section", "ctx", "dp"),
        P("section", "ctx", "dp"),
        P("section", "ctx", "dp"),
        P("section", "dp", "ctx"),
        P("section", None),
        P("section", "ctx", None),
    )
    return jax.shard_map(
        local,
        mesh=mesh,
        in_specs=placed,
        out_specs=(
            P("section", "ctx", "dp"),
            P("section", "ctx", "dp"),
            P("section", "ctx", "dp"),
            P("section", ("dp", "ctx"), None),
        ),
        check_vma=False,
    )
```

```python
import functools

import jax
import jax.numpy as jnp
from jax import lax
from jax.experimental import pallas as pl
from jax.experimental.pallas import tpu as pltpu
from jax.sharding import PartitionSpec as P

QH = 64
KVH = 8
HD = 128
GROUP = QH // KVH
LOG2E = 1.4426950408889634
KT = 256
BQ = 256
ROWS = GROUP * BQ
WIDTH = GROUP * HD
MESH = pl.DeviceIdType.MESH


def attn_kernel(own, resume, final, slots, tok, *refs):
    refs = list(refs)
    bounds = refs.pop(0)
    q_ref, do_ref, lse_ref, delta_ref, beg_ref = (refs.pop(0) for _ in range(5))
    if own:
        k_ref, v_ref = refs.pop(0), refs.pop(0)
    else:
        kv_refs = [refs.pop(0) for _ in range(slots)]
    dq_in = refs.pop(0) if resume else None
    dq_ref = refs.pop(0)
    grads = [refs.pop(0) for _ in range(slots)]
    dkacc, dvacc, qs, dos, dqacc = (refs.pop(0) for _ in range(5))
    if not own:
        k_ref, v_ref = refs.pop(0), refs.pop(0)

    step = pl.program_id(0)
    scale = HD ** -0.5
    base = 0 if own else slots * tok
    row0 = base + step * BQ

    @pl.when(step == 0)
    def _():
        if not own:
            for slot, ref in enumerate(kv_refs):
                k_ref[slot * tok:(slot + 1) * tok, :] = ref[:, :HD]
                v_ref[slot * tok:(slot + 1) * tok, :] = ref[:, HD:]
        dkacc[...] = jnp.zeros_like(dkacc)
        dvacc[...] = jnp.zeros_like(dvacc)

    for h in range(GROUP):
        qs[h * BQ:(h + 1) * BQ, :] = q_ref[:, h * HD:(h + 1) * HD]
        dos[h * BQ:(h + 1) * BQ, :] = do_ref[:, h * HD:(h + 1) * HD]
    dqacc[...] = dq_in[0] if resume else jnp.zeros_like(dqacc)

    def tile(pair, masked):
        start = pl.multiple_of(pair * KT, KT)
        k = k_ref[pl.ds(start, KT), :]
        kt = k.T
        v = v_ref[pl.ds(start, KT), :]
        q = qs[...]
        g = dos[...]
        s = lax.dot_general(k, q, (((1,), (1,)), ((), ())), preferred_element_type=jnp.float32)
        p = jnp.exp2(s * (scale * LOG2E) - lse_ref[0, 0])
        if masked:
            u = lax.broadcasted_iota(jnp.int32, (KT, ROWS), 0) + start
            allowed = u >= beg_ref[0]
            if own:
                t = (lax.broadcasted_iota(jnp.int32, (1, ROWS), 1) & (BQ - 1)) + row0
                allowed &= u <= t
            p = jnp.where(allowed, p, 0.0)
        dp = lax.dot_general(v, g, (((1,), (1,)), ((), ())), preferred_element_type=jnp.float32)
        ds = (p * (dp - delta_ref[0, 0])).astype(jnp.bfloat16)
        pb = p.astype(jnp.bfloat16)
        dvacc[pl.ds(start, KT), :] += jnp.dot(pb, g, preferred_element_type=jnp.float32)
        dkacc[pl.ds(start, KT), :] += jnp.dot(ds, q, preferred_element_type=jnp.float32)
        dqacc[...] += jnp.dot(kt, ds, preferred_element_type=jnp.float32)

    lo = bounds[0, step]
    mid = bounds[1, step]
    last = bounds[2, step]
    edge = mid - lo

    def masked_step(i, carry):
        tile(jnp.where(i < edge, lo + i, last), True)
        return carry

    def plain_step(i, carry):
        tile(i, False)
        return carry

    lax.fori_loop(0, edge + 1 if own else edge, masked_step, 0)
    lax.fori_loop(mid, last, plain_step, 0)

    if final:
        for h in range(GROUP):
            dq_ref[0, :, h * HD:(h + 1) * HD] = (dqacc[:, h * BQ:(h + 1) * BQ].T * scale).astype(jnp.bfloat16)
    else:
        dq_ref[0] = dqacc[...]

    @pl.when(step == pl.num_programs(0) - 1)
    def _():
        for slot, ref in enumerate(grads):
            at = slice(slot * tok, (slot + 1) * tok)
            ref[0] = dvacc[at, :].astype(jnp.bfloat16)
            ref[1] = (dkacc[at, :] * scale).astype(jnp.bfloat16)


def attention(head, own, bounds, q, do, lse, delta, beg, kv, dq_in, final):
    tok, width = q.shape
    blocks = tok // BQ
    slots = 1 if own else 2
    spec_q = pl.BlockSpec((BQ, WIDTH), lambda i, *_: (i, head))
    spec_row = pl.BlockSpec((1, 1, 1, ROWS), lambda i, *_: (head, i, 0, 0))
    spec_acc = pl.BlockSpec((1, HD, ROWS), lambda i, *_: (i, 0, 0))
    spec_grad = pl.BlockSpec((2, tok, HD), lambda i, *_: (0, 0, 0))
    in_specs = [spec_q, spec_q, spec_row, spec_row, pl.BlockSpec((1, 1, ROWS), lambda i, *_: (i, 0, 0))]
    args = [q, do, lse, delta, beg]
    if own:
        in_specs += [pl.BlockSpec((tok, HD), lambda i, *_: (0, head))] * 2
    else:
        in_specs += [pl.BlockSpec((tok, 2 * HD), lambda i, *_: (0, 0))] * 2
    args += list(kv)
    if dq_in is not None:
        in_specs.append(spec_acc)
        args.append(dq_in)
    if final:
        dq_shape = jax.ShapeDtypeStruct((1, tok, WIDTH), jnp.bfloat16)
        dq_spec = pl.BlockSpec((1, BQ, WIDTH), lambda i, *_: (0, i, 0))
    else:
        dq_shape, dq_spec = jax.ShapeDtypeStruct((blocks, HD, ROWS), jnp.float32), spec_acc
    scratch = [
        pltpu.VMEM((slots * tok, HD), jnp.float32),
        pltpu.VMEM((slots * tok, HD), jnp.float32),
        pltpu.VMEM((ROWS, HD), jnp.bfloat16),
        pltpu.VMEM((ROWS, HD), jnp.bfloat16),
        pltpu.VMEM((HD, ROWS), jnp.float32),
    ]
    if not own:
        scratch += [pltpu.VMEM((slots * tok, HD), jnp.bfloat16)] * 2
    pairs = 10 if own else 22
    out = pl.pallas_call(
        functools.partial(attn_kernel, own, dq_in is not None, final, slots, tok),
        out_shape=[dq_shape] + [jax.ShapeDtypeStruct((2, tok, HD), jnp.bfloat16)] * slots,
        grid_spec=pltpu.PrefetchScalarGridSpec(
            num_scalar_prefetch=1,
            grid=(blocks,),
            in_specs=in_specs,
            out_specs=[dq_spec] + [spec_grad] * slots,
            scratch_shapes=scratch,
        ),
        compiler_params=pltpu.CompilerParams(
            dimension_semantics=("arbitrary",), vmem_limit_bytes=54 << 20),
        cost_estimate=pl.CostEstimate(
            flops=pairs * 10 * KT * ROWS * HD, transcendentals=pairs * KT * ROWS,
            bytes_accessed=10 << 20),
        name="attn_own" if own else "attn_far",
    )(bounds, *args)
    return out[0], list(out[1:])


def block_tables(starts, shard, tok):
    blocks = tok // BQ
    pos = shard * tok + jnp.arange(tok, dtype=jnp.int32)
    begin = jnp.max(jnp.where(starts[None, :] <= pos[:, None], starts[None, :], 0), axis=1)
    begin = (begin - (shard - 2) * tok).reshape(blocks, BQ)
    edge = 2 * tok // KT
    last = edge + jnp.arange(blocks, dtype=jnp.int32) * BQ // KT
    lo = begin[:, 0] // KT
    mid = jnp.minimum((begin[:, -1] + KT - 1) // KT, last)
    far = jnp.stack([jnp.minimum(lo, edge), jnp.minimum(mid, edge), jnp.full_like(lo, edge)])
    near = jnp.stack([jnp.maximum(lo, edge), jnp.maximum(mid, edge), last]) - edge
    beg = jnp.tile(begin, (1, GROUP)).reshape(blocks, 1, ROWS)
    return far.astype(jnp.int32), near.astype(jnp.int32), beg, beg - 2 * tok


def rows_kernel(do_ref, o_ref, lse_ref, delta_ref, lse2_ref):
    heads = lse_ref.shape[0]
    lane = lax.broadcasted_iota(jnp.int32, (2 * HD, HD), 1)
    total = None
    for n in range(heads):
        at = slice(n * HD, (n + 1) * HD)
        prod = do_ref[:, at].astype(jnp.float32) * o_ref[:, at].astype(jnp.float32)
        high = prod.astype(jnp.bfloat16)
        low = (prod - high.astype(jnp.float32)).astype(jnp.bfloat16)
        pick = jnp.where(lane == n, 1.0, 0.0).astype(jnp.bfloat16)
        part = jnp.dot(jnp.concatenate([high, low], axis=1), pick, preferred_element_type=jnp.float32)
        total = part if total is None else total + part
    total = total.T
    for n in range(heads):
        to = slice(n % GROUP * BQ, (n % GROUP + 1) * BQ)
        delta_ref[n // GROUP, 0, :, to] = total[n:n + 1, :]
        lse2_ref[n // GROUP, 0, :, to] = lse_ref[n:n + 1, :] * LOG2E


def row_tables(do, o, lse):
    tok, width = do.shape
    heads = lse.shape[0]
    kv_local = heads // GROUP
    blocks = tok // BQ
    spec = pl.BlockSpec((BQ, width), lambda i: (i, 0))
    spec_row = pl.BlockSpec((kv_local, 1, 1, ROWS), lambda i: (0, i, 0, 0))
    return pl.pallas_call(
        rows_kernel,
        out_shape=[jax.ShapeDtypeStruct((kv_local, blocks, 1, ROWS), jnp.float32)] * 2,
        grid=(blocks,),
        in_specs=[spec, spec, pl.BlockSpec((heads, BQ), lambda i: (0, i))],
        out_specs=[spec_row, spec_row],
        compiler_params=pltpu.CompilerParams(
            dimension_semantics=("arbitrary",), vmem_limit_bytes=58 << 20),
        cost_estimate=pl.CostEstimate(
            flops=4 * tok * width, transcendentals=0, bytes_accessed=4 * tok * width),
        name="row_tables",
    )(do, o, lse)


def ctx_send(array, by):
    n = lax.axis_size("ctx")
    return lax.ppermute(array, "ctx", [(i, i + by) for i in range(n) if 0 <= i + by < n])


def home(array, by):
    n = lax.axis_size("ctx")
    m = lax.axis_size("section")
    pairs = [(s * n + i, (s - 1) % m * n + i - by)
             for s in range(m) for i in range(n) if i - by >= 0]
    return lax.ppermute(array, ("section", "ctx"), pairs)


def tail_kernel(nd, nc, ns, wscale, kv_local, *refs):
    refs = list(refs)
    take = lambda n: [refs.pop(0) for _ in range(n)]
    last = kv_local - 1
    before_parts = [take(3) for _ in range(last)]
    (far2, far1, lse_ref, delta_ref, beg_ref, k_ref, v_ref, q_hbm, do_hbm, dq_hbm, feat_hbm,
     w_ref, vg_ref, kg_ref, dq_ref,
     feat, qv, gv, dqv, qs, dos, pbuf, dqs, dkacc, dvacc, own, landed, back, dvall, dts,
     send, recv, acc, send1, recv1, send2, recv2, acc2,
     lsem, osend, orecv, bsend, brecv, asend, arecv, rsend, rrecv, tsend, trecv, qsend, qrecv) = refs
    z = lax.axis_index("dp")
    c = lax.axis_index("ctx")
    s = lax.axis_index("section")
    scale = HD ** -0.5
    tok = k_ref.shape[0]
    rows = w_ref.shape[0]
    steps = tok // BQ
    cols = slice(last * HD, (last + 1) * HD)
    wide = pl.ds(last * WIDTH, WIDTH)

    loads = [
        pltpu.make_async_copy(src, dst, lsem.at[i])
        for i, (src, dst) in enumerate((
            (q_hbm.at[:, wide], qv), (do_hbm.at[:, wide], gv), (dq_hbm, dqv), (feat_hbm, feat)))]
    for copy in loads:
        copy.start()

    has_up = z + 1 < nd
    has_down = z >= 1
    to = lax.rem(s + ns - 1, ns)
    come = lax.rem(s + 1, ns)
    barrier = pltpu.get_barrier_semaphore()

    def greet(**device):
        pl.semaphore_signal(barrier, inc=1, device_id=device, device_id_type=MESH)

    col, row = lax.rem(c, 2), c // 2
    across = (row * 2 + 1 - col, (1 - row) * 2 + col)
    for j in range(1, nc):
        greet(ctx=lax.rem(c + j, nc))
    greet(section=come)
    for by in (1, 2):
        @pl.when(c + by < nc)
        def _():
            greet(section=come, ctx=c + by)

    @pl.when(has_up)
    def _():
        greet(dp=z + 1)

    @pl.when(has_down)
    def _():
        greet(dp=z - 1)

    one = lambda cond: jnp.where(cond, 1, 0)
    pl.semaphore_wait(barrier, nc + one(c >= 1) + one(c >= 2) + one(has_up) + one(has_down))

    def hand(src, head, kind):
        return pltpu.make_async_remote_copy(
            src_ref=src.at[kind], dst_ref=landed.at[head, kind],
            send_sem=osend.at[head, kind], recv_sem=orecv.at[head, kind],
            device_id={"section": to}, device_id_type=MESH)

    def partial_home(src, by, kind):
        return pltpu.make_async_remote_copy(
            src_ref=src.at[kind], dst_ref=back.at[by - 1, kind],
            send_sem=bsend.at[by - 1, kind], recv_sem=brecv.at[by - 1, kind],
            device_id={"section": to, "ctx": c - by}, device_id_type=MESH)

    def send_back(kind):
        for by, src in ((2, far2), (1, far1)):
            @pl.when(c >= by)
            def _():
                partial_home(src, by, kind).start()

            @pl.when(c + by >= nc)
            def _():
                back[by - 1, kind] = jnp.zeros((tok, HD), jnp.bfloat16)

    for head in range(last):
        hand(before_parts[head][0], head, 0).start()
    send_back(0)
    for head in range(last):
        hand(before_parts[head][0], head, 1).start()

    def hop(head, src, way, k):
        return pltpu.make_async_remote_copy(
            src_ref=dvall.at[head, src], dst_ref=dvall.at[head, src],
            send_sem=asend.at[head, way, k], recv_sem=arecv.at[head, src],
            device_id={"dp": z + 1 if way == 0 else z - 1}, device_id_type=MESH)

    def each_hop(head, k, act):
        up, down = z - k, z + k

        @pl.when((up >= 0) & has_up)
        def _():
            act(hop(head, up, 0, k))

        @pl.when((down < nd) & has_down)
        def _():
            act(hop(head, down, 1, k))

    def share(j, src):
        return pltpu.make_async_remote_copy(
            src_ref=send.at[j - 1, src], dst_ref=recv.at[j - 1, src],
            send_sem=rsend.at[j - 1, src], recv_sem=rrecv.at[j - 1, src],
            device_id={"ctx": lax.rem(c + j, nc)}, device_id_type=MESH)

    def fold(phase, head, src):
        a, b = ((send1, recv1), (send2, recv2))[phase]
        return pltpu.make_async_remote_copy(
            src_ref=a.at[head, src], dst_ref=b.at[head, src],
            send_sem=tsend.at[phase, head, src], recv_sem=trecv.at[phase, head, src],
            device_id={"ctx": across[phase]}, device_id_type=MESH)

    def product(target):
        return jnp.dot(dts[...], feat[:, pl.ds(pl.multiple_of(target * rows, 128), rows)],
                       preferred_element_type=jnp.float32)

    def process(head, src):
        dts[...] = dvall[head, src].T
        if head == last:
            for j in range(1, nc):
                send[j - 1, src] = product(lax.rem(c + j, nc)).astype(jnp.bfloat16)
                share(j, src).start()
            acc[src] = product(c)
        else:
            for y in (0, 1):
                send1[head, src, y] = product(y * 2 + 1 - col).astype(jnp.bfloat16)
            fold(0, head, src).start()
            for y in (0, 1):
                acc2[head, src, y] = product(y * 2 + col)

    def settle_one(head, src):
        fold(0, head, src).wait_recv()
        away = 1 - row
        send2[head, src] = (acc2[head, src, away] + recv1[head, src, away]).astype(jnp.bfloat16)
        fold(1, head, src).start()

    def settle(head, k):
        if k == 0:
            settle_one(head, z)
        else:
            for src, cond in ((z - k, z >= k), (z + k, z + k < nd)):
                @pl.when(cond)
                def _():
                    settle_one(head, src)

    def weights(head):
        for src in range(nd):
            if head == last:
                total = acc[src]
                for j in range(1, nc):
                    share(j, src).wait_recv()
                    total = total + recv[j - 1, src]
            else:
                fold(1, head, src).wait_recv()
                total = acc2[head, src, row] + recv1[head, src, row] + recv2[head, src]
            at = (src * kv_local + head) * HD
            w_ref[:, at:at + HD] = total.T * wscale

    def advance(head, k):
        up, down = z - k, z + k

        @pl.when(up >= 0)
        def _():
            hop(head, up, 0, 0).wait_recv()

        @pl.when(down < nd)
        def _():
            hop(head, down, 1, 0).wait_recv()

        if k < nd - 1:
            each_hop(head, k, lambda copy: copy.start())

        @pl.when(up >= 0)
        def _():
            process(head, up)

        @pl.when(down < nd)
        def _():
            process(head, down)

    def begin(head, two, one):
        at = slice(head * HD, (head + 1) * HD)
        total = (landed[head, 0].astype(jnp.float32) + two[0] + one[0]).astype(jnp.bfloat16)
        dvall[head, z] = total
        each_hop(head, 0, lambda copy: copy.start())
        vg_ref[:, at] = total

    def send_dq(i):
        at = pl.ds(i * BQ, BQ)
        return pltpu.make_async_remote_copy(
            src_ref=dqs.at[at], dst_ref=dq_ref.at[at], send_sem=qsend.at[i], recv_sem=qrecv.at[i],
            device_id={"section": to}, device_id_type=MESH)

    def stack_rows(i):
        for h in range(GROUP):
            qs[h * BQ:(h + 1) * BQ, :] = qv[i * BQ:(i + 1) * BQ, h * HD:(h + 1) * HD]
            dos[h * BQ:(h + 1) * BQ, :] = gv[i * BQ:(i + 1) * BQ, h * HD:(h + 1) * HD]

    def attend_values(i):
        stack_rows(i)

        def tile(pair, carry):
            start = pl.multiple_of(pair * KT, KT)
            k = k_ref[pl.ds(start, KT), cols]
            sc = lax.dot_general(k, qs[...], (((1,), (1,)), ((), ())), preferred_element_type=jnp.float32)
            p = jnp.exp2(sc * (scale * LOG2E) - lse_ref[last, i])
            u = lax.broadcasted_iota(jnp.int32, (KT, ROWS), 0) + start
            t = (lax.broadcasted_iota(jnp.int32, (1, ROWS), 1) & (BQ - 1)) + i * BQ
            pb = jnp.where((u >= beg_ref[i]) & (u <= t), p, 0.0).astype(jnp.bfloat16)
            pbuf[i * (i + 1) // 2 + pair] = pb
            dvacc[pl.ds(start, KT), :] += jnp.dot(pb, dos[...], preferred_element_type=jnp.float32)
            return carry

        lax.fori_loop(0, i + 1, tile, 0)

    def attend_scores(i):
        stack_rows(i)

        def tile(pair, carry):
            start = pl.multiple_of(pair * KT, KT)
            kt = k_ref[pl.ds(start, KT), cols].T
            v = v_ref[pl.ds(start, KT), cols]
            p = pbuf[i * (i + 1) // 2 + pair].astype(jnp.float32)
            dp = lax.dot_general(v, dos[...], (((1,), (1,)), ((), ())), preferred_element_type=jnp.float32)
            ds = (p * (dp - delta_ref[last, i])).astype(jnp.bfloat16)
            dkacc[pl.ds(start, KT), :] += jnp.dot(ds, qs[...], preferred_element_type=jnp.float32)
            dqv[i] += jnp.dot(kt, ds, preferred_element_type=jnp.float32)
            return carry

        lax.fori_loop(0, i + 1, tile, 0)
        for h in range(GROUP):
            dqs[i * BQ:(i + 1) * BQ, h * HD:(h + 1) * HD] = (
                dqv[i, :, h * BQ:(h + 1) * BQ].T * scale).astype(jnp.bfloat16)
        send_dq(i).start()

    dkacc[...] = jnp.zeros_like(dkacc)
    dvacc[...] = jnp.zeros_like(dvacc)
    for head in range(last):
        hand(before_parts[head][0], head, 0).wait_recv()
        begin(head, before_parts[head][1], before_parts[head][2])
    loads[0].wait()
    loads[1].wait()
    attend_values(steps - 1)
    loads[3].wait()
    for head in range(last):
        process(head, z)
    for i in reversed(range(steps - 1)):
        attend_values(i)
        if i == steps - 2:
            for head in range(last):
                advance(head, 1)
                settle(head, 0)
    own[0] = dvacc[...].astype(jnp.bfloat16)
    hand(own, last, 0).start()
    for by in (2, 1):
        @pl.when(c + by < nc)
        def _():
            partial_home(far1, by, 0).wait_recv()
    hand(own, last, 0).wait_recv()
    begin(last, back.at[1], back.at[0])
    send_back(1)
    process(last, z)
    loads[2].wait()
    todo = []
    for k in range(2, nd):
        for head in range(last):
            todo += [(advance, head, k), (settle, head, k - 1)]
        if k < nd - 1:
            todo += [(advance, last, k - 1)]
    todo += [(advance, last, nd - 2)]
    todo += [(settle, head, nd - 1) for head in range(last)]

    def run(n):
        for act, head, k in todo[:n]:
            act(head, k)
        del todo[:n]

    for i in reversed(range(steps)):
        attend_scores(i)
        if i == 0:
            own[1] = (dkacc[...] * scale).astype(jnp.bfloat16)
            hand(own, last, 1).start()
        run(2 if i == steps - 1 else 1)
    run(len(todo))
    for head in range(last):
        weights(head)
    for head in range(kv_local):
        if head == last:
            for by in (2, 1):
                @pl.when(c + by < nc)
                def _():
                    partial_home(far1, by, 1).wait_recv()
            two, one_ref = back.at[1], back.at[0]
            hand(own, head, 1).wait_recv()
        else:
            two, one_ref = before_parts[head][1:]
            hand(before_parts[head][0], head, 1).wait_recv()
        kg_ref[:, head * HD:(head + 1) * HD] = (
            landed[head, 1].astype(jnp.float32) + two[1] + one_ref[1]).astype(jnp.bfloat16)
    advance(last, nd - 1)
    for head in range(kv_local):
        for kind in (0, 1):
            hand(own if head == last else before_parts[head][0], head, kind).wait_send()
        for k in range(nd - 1):
            each_hop(head, k, lambda copy: copy.wait_send())
    for kind in (0, 1):
        for by, src in ((2, far2), (1, far1)):
            @pl.when(c >= by)
            def _():
                partial_home(src, by, kind).wait_send()
    for i in range(steps):
        send_dq(i).wait()
    weights(last)

    def drain(i, carry):
        for j in range(1, nc):
            share(j, i).wait_send()
        for head in range(last):
            for phase in (0, 1):
                fold(phase, head, i).wait_send()
        return carry

    lax.fori_loop(0, nd, drain, 0)


def tail(feat, q, do, k, v, lse, delta, beg, parts, far, dq, nd, nc, ns, scale):
    tok, width = feat.shape
    rows = width // nc
    kv_local = len(parts) + 1
    others = max(len(parts), 1)
    steps = tok // BQ
    bf16, f32 = jnp.bfloat16, jnp.float32
    vmem, dma = pltpu.VMEM, pltpu.SemaphoreType.DMA
    whole = pl.BlockSpec(memory_space=pltpu.VMEM)
    return pl.pallas_call(
        functools.partial(tail_kernel, nd, nc, ns, scale, kv_local),
        out_shape=[
            jax.ShapeDtypeStruct((rows, nd * kv_local * HD), f32),
            jax.ShapeDtypeStruct((tok, kv_local * HD), bf16),
            jax.ShapeDtypeStruct((tok, kv_local * HD), bf16),
            jax.ShapeDtypeStruct((tok, WIDTH), bf16),
        ],
        in_specs=[whole] * (3 * len(parts) + 7) + [pl.BlockSpec(memory_space=pl.ANY)] * 4,
        out_specs=[whole] * 3 + [pl.BlockSpec(memory_space=pl.ANY)],
        scratch_shapes=[
            vmem((tok, width), bf16),
            vmem((tok, WIDTH), bf16),
            vmem((tok, WIDTH), bf16),
            vmem((steps, HD, ROWS), f32),
            vmem((ROWS, HD), bf16),
            vmem((ROWS, HD), bf16),
            vmem((steps * (steps + 1) // 2, KT, ROWS), bf16),
            vmem((tok, WIDTH), bf16),
            vmem((tok, HD), f32),
            vmem((tok, HD), f32),
            vmem((2, tok, HD), bf16),
            vmem((kv_local, 2, tok, HD), bf16),
            vmem((2, 2, tok, HD), bf16),
            vmem((kv_local, nd, tok, HD), bf16),
            vmem((HD, tok), bf16),
            vmem((nc - 1, nd, HD, rows), bf16),
            vmem((nc - 1, nd, HD, rows), bf16),
            vmem((nd, HD, rows), f32),
            vmem((others, nd, 2, HD, rows), bf16),
            vmem((others, nd, 2, HD, rows), bf16),
            vmem((others, nd, HD, rows), bf16),
            vmem((others, nd, HD, rows), bf16),
            vmem((others, nd, 2, HD, rows), f32),
            dma((4,)),
            dma((kv_local, 2)),
            dma((kv_local, 2)),
            dma((2, 2)),
            dma((2, 2)),
            dma((kv_local, 2, nd)),
            dma((kv_local, nd)),
            dma((nc - 1, nd)),
            dma((nc - 1, nd)),
            dma((2, others, nd)),
            dma((2, others, nd)),
            dma((steps,)),
            dma((steps,)),
        ],
        compiler_params=pltpu.CompilerParams(
            collective_id=0, has_side_effects=True, vmem_limit_bytes=62 << 20),
        cost_estimate=pl.CostEstimate(
            flops=2 * tok * width * nd * kv_local * HD + 10 * 10 * KT * ROWS * HD,
            transcendentals=10 * KT * ROWS, bytes_accessed=20 << 20),
        name="tail",
    )(*[part for head in parts for part in head], *far, lse, delta, beg, k, v, q, do, dq, feat)


def finish_kernel(*refs):
    *parts, weight, value, key, dq_out, w_out, v_out, k_out = refs
    width = parts[0].shape[2]
    for i, part in enumerate(parts):
        dq_out[:, :, i * width:(i + 1) * width] = part[...]
    w_out[0] = weight[...]
    v_out[0] = value[...]
    k_out[0] = key[...]


def finish(dq_parts, weight, value, key):
    _, tok, width = dq_parts[0].shape
    n = 4
    cut = lambda a: pl.BlockSpec((a.shape[0] // n, a.shape[1]), lambda i: (i, 0))
    cut3 = lambda a: pl.BlockSpec((1, a.shape[0] // n, a.shape[1]), lambda i: (0, i, 0))
    wide = lambda w: pl.BlockSpec((1, tok // n, w), lambda i: (0, i, 0))
    return pl.pallas_call(
        finish_kernel,
        out_shape=[
            jax.ShapeDtypeStruct((1, tok, width * len(dq_parts)), jnp.bfloat16),
            jax.ShapeDtypeStruct((1, *weight.shape), weight.dtype),
            jax.ShapeDtypeStruct((1, *value.shape), value.dtype),
            jax.ShapeDtypeStruct((1, *key.shape), key.dtype),
        ],
        grid=(n,),
        in_specs=[wide(width)] * len(dq_parts) + [cut(weight), cut(value), cut(key)],
        out_specs=[wide(width * len(dq_parts)), cut3(weight), cut3(value), cut3(key)],
        compiler_params=pltpu.CompilerParams(
            dimension_semantics=("arbitrary",), vmem_limit_bytes=50 << 20),
        name="finish",
    )(*dq_parts, weight, value, key)


def weight_plain(feat, dv, nd, nc, scale):
    shard = lax.axis_index("ctx")
    rows = feat.shape[1] // nc
    dv_all = lax.all_gather(dv, "dp", axis=1, tiled=True)

    def partial(target):
        cols = lax.dynamic_slice_in_dim(feat, target * rows, rows, 1)
        return lax.dot_general(cols, dv_all, (((0,), (0,)), ((), ())),
                               preferred_element_type=jnp.float32)

    total = partial(shard)
    for by in range(1, nc):
        sent = partial((shard + by) % nc).astype(jnp.bfloat16)
        total = total + lax.ppermute(sent, "ctx", [(i, (i + by) % nc) for i in range(nc)])
    return total * scale


def local(features, queries, keys, values, attn_out, out_grad, lse, doc_starts, key_blocks):
    tok = queries.shape[1]
    kv_local = keys.shape[2] // HD
    shard = lax.axis_index("ctx")
    nc = lax.axis_size("ctx")
    nd = lax.axis_size("dp")
    ns = lax.axis_size("section")
    q, do, k, v = queries[0], out_grad[0], keys[0], values[0]

    def window(head):
        return ctx_send(packed[head], 2), ctx_send(packed[head], 1)

    packed = [jnp.concatenate([k[:, head * HD:(head + 1) * HD], v[:, head * HD:(head + 1) * HD]], axis=1)
              for head in range(kv_local)]
    windows = [window(0)]
    far, near, beg_far, beg_near = block_tables(doc_starts[0], shard, tok)
    delta, lse2 = row_tables(do, attn_out[0], lse[0])
    scale = (tok * nc) ** -0.5
    feat = features[0]
    last = kv_local - 1
    dq_parts, parts = [], []
    for head in range(last):
        dq, (own,) = attention(head, True, near, q, do, lse2, delta, beg_near, (k, v), None, False)
        packed[head + 1], _ = lax.optimization_barrier((packed[head + 1], own))
        windows.append(window(head + 1))
        dq, (two, one) = attention(head, False, far, q, do, lse2, delta, beg_far, windows[head], dq, True)
        far, _ = lax.optimization_barrier((far, two))
        dq_parts.append(home(dq, 0))
        parts.append((own, home(two, 2), home(one, 1)))
    dq, (two, one) = attention(last, False, far, q, do, lse2, delta, beg_far, windows[last], None, False)
    if nc == 4 and feat.shape[1] // nc % 128 == 0:
        weight, value_grad, key_grad, dq = tail(
            feat, q, do, k, v, lse2, delta, beg_near, parts, (two, one), dq, nd, nc, ns, scale)
        dq_parts.append(dq[None])
        query_grad, weight, value_grad, key_grad = finish(dq_parts, weight, value_grad, key_grad)
        return query_grad, key_grad, value_grad, weight
    else:
        dq, (own,) = attention(last, True, near, q, do, lse2, delta, beg_near, (k, v), dq, True)
        dq_parts.append(home(dq, 0))
        parts.append((own, home(two, 2), home(one, 1)))
        grads = [(home(own, 0).astype(jnp.float32) + two + one).astype(jnp.bfloat16) for own, two, one in parts]
        value_grad = jnp.concatenate([grad[0] for grad in grads], axis=1)
        key_grad = jnp.concatenate([grad[1] for grad in grads], axis=1)
        weight = weight_plain(feat, value_grad, nd, nc, scale)
    query_grad = jnp.concatenate(dq_parts, axis=2)
    return query_grad, key_grad[None], value_grad[None], weight[None]


def solution(mesh):
    placed = (
        P("section", "ctx", "dp"),
        P("section", "ctx", "dp"),
        P("section", "ctx", "dp"),
        P("section", "ctx", "dp"),
        P("section", "ctx", "dp"),
        P("section", "ctx", "dp"),
        P("section", "dp", "ctx"),
        P("section", None),
        P("section", "ctx", None),
    )
    return jax.shard_map(
        local,
        mesh=mesh,
        in_specs=placed,
        out_specs=(
            P("section", "ctx", "dp"),
            P("section", "ctx", "dp"),
            P("section", "ctx", "dp"),
            P("section", ("dp", "ctx"), None),
        ),
        check_vma=False,
    )
```

```python
import functools

import jax
import jax.numpy as jnp
from jax import lax
from jax.experimental import pallas as pl
from jax.experimental.pallas import tpu as pltpu
from jax.sharding import PartitionSpec as P

QH = 64
KVH = 8
HD = 128
GROUP = QH // KVH
LOG2E = 1.4426950408889634
KT = 256
BQ = 256
ROWS = GROUP * BQ
WIDTH = GROUP * HD
MESH = pl.DeviceIdType.MESH


def attn_kernel(own, resume, final, slots, tok, *refs):
    refs = list(refs)
    bounds = refs.pop(0)
    q_ref, do_ref, lse_ref, delta_ref, beg_ref = (refs.pop(0) for _ in range(5))
    if own:
        k_ref, v_ref = refs.pop(0), refs.pop(0)
    else:
        kv_refs = [refs.pop(0) for _ in range(slots)]
    dq_in = refs.pop(0) if resume else None
    dq_ref = refs.pop(0)
    grads = [refs.pop(0) for _ in range(slots)]
    dkacc, dvacc, qs, dos, dqacc = (refs.pop(0) for _ in range(5))
    if not own:
        k_ref, v_ref = refs.pop(0), refs.pop(0)

    step = pl.program_id(0)
    scale = HD ** -0.5
    base = 0 if own else slots * tok
    row0 = base + step * BQ

    @pl.when(step == 0)
    def _():
        if not own:
            for slot, ref in enumerate(kv_refs):
                k_ref[slot * tok:(slot + 1) * tok, :] = ref[:, :HD]
                v_ref[slot * tok:(slot + 1) * tok, :] = ref[:, HD:]
        dkacc[...] = jnp.zeros_like(dkacc)
        dvacc[...] = jnp.zeros_like(dvacc)

    for h in range(GROUP):
        qs[h * BQ:(h + 1) * BQ, :] = q_ref[:, h * HD:(h + 1) * HD]
        dos[h * BQ:(h + 1) * BQ, :] = do_ref[:, h * HD:(h + 1) * HD]
    dqacc[...] = dq_in[0] if resume else jnp.zeros_like(dqacc)

    def tile(pair, masked):
        start = pl.multiple_of(pair * KT, KT)
        k = k_ref[pl.ds(start, KT), :]
        kt = k.T
        v = v_ref[pl.ds(start, KT), :]
        q = qs[...]
        g = dos[...]
        s = lax.dot_general(k, q, (((1,), (1,)), ((), ())), preferred_element_type=jnp.float32)
        p = jnp.exp2(s * (scale * LOG2E) - lse_ref[0, 0])
        if masked:
            u = lax.broadcasted_iota(jnp.int32, (KT, ROWS), 0) + start
            allowed = u >= beg_ref[0]
            if own:
                t = (lax.broadcasted_iota(jnp.int32, (1, ROWS), 1) & (BQ - 1)) + row0
                allowed &= u <= t
            p = jnp.where(allowed, p, 0.0)
        dp = lax.dot_general(v, g, (((1,), (1,)), ((), ())), preferred_element_type=jnp.float32)
        ds = (p * (dp - delta_ref[0, 0])).astype(jnp.bfloat16)
        pb = p.astype(jnp.bfloat16)
        dvacc[pl.ds(start, KT), :] += jnp.dot(pb, g, preferred_element_type=jnp.float32)
        dkacc[pl.ds(start, KT), :] += jnp.dot(ds, q, preferred_element_type=jnp.float32)
        dqacc[...] += jnp.dot(kt, ds, preferred_element_type=jnp.float32)

    lo = bounds[0, step]
    mid = bounds[1, step]
    last = bounds[2, step]
    edge = mid - lo

    def masked_step(i, carry):
        tile(jnp.where(i < edge, lo + i, last), True)
        return carry

    def plain_step(i, carry):
        tile(i, False)
        return carry

    lax.fori_loop(0, edge + 1 if own else edge, masked_step, 0)
    lax.fori_loop(mid, last, plain_step, 0)

    if final:
        for h in range(GROUP):
            dq_ref[0, :, h * HD:(h + 1) * HD] = (dqacc[:, h * BQ:(h + 1) * BQ].T * scale).astype(jnp.bfloat16)
    else:
        dq_ref[0] = dqacc[...]

    @pl.when(step == pl.num_programs(0) - 1)
    def _():
        for slot, ref in enumerate(grads):
            at = slice(slot * tok, (slot + 1) * tok)
            ref[0] = dvacc[at, :].astype(jnp.bfloat16)
            ref[1] = (dkacc[at, :] * scale).astype(jnp.bfloat16)


def attention(head, own, bounds, q, do, lse, delta, beg, kv, dq_in, final):
    tok, width = q.shape
    blocks = tok // BQ
    slots = 1 if own else 2
    spec_q = pl.BlockSpec((BQ, WIDTH), lambda i, *_: (i, head))
    spec_row = pl.BlockSpec((1, 1, 1, ROWS), lambda i, *_: (head, i, 0, 0))
    spec_acc = pl.BlockSpec((1, HD, ROWS), lambda i, *_: (i, 0, 0))
    spec_grad = pl.BlockSpec((2, tok, HD), lambda i, *_: (0, 0, 0))
    in_specs = [spec_q, spec_q, spec_row, spec_row, pl.BlockSpec((1, 1, ROWS), lambda i, *_: (i, 0, 0))]
    args = [q, do, lse, delta, beg]
    if own:
        in_specs += [pl.BlockSpec((tok, HD), lambda i, *_: (0, head))] * 2
    else:
        in_specs += [pl.BlockSpec((tok, 2 * HD), lambda i, *_: (0, 0))] * 2
    args += list(kv)
    if dq_in is not None:
        in_specs.append(spec_acc)
        args.append(dq_in)
    if final:
        dq_shape = jax.ShapeDtypeStruct((1, tok, WIDTH), jnp.bfloat16)
        dq_spec = pl.BlockSpec((1, BQ, WIDTH), lambda i, *_: (0, i, 0))
    else:
        dq_shape, dq_spec = jax.ShapeDtypeStruct((blocks, HD, ROWS), jnp.float32), spec_acc
    scratch = [
        pltpu.VMEM((slots * tok, HD), jnp.float32),
        pltpu.VMEM((slots * tok, HD), jnp.float32),
        pltpu.VMEM((ROWS, HD), jnp.bfloat16),
        pltpu.VMEM((ROWS, HD), jnp.bfloat16),
        pltpu.VMEM((HD, ROWS), jnp.float32),
    ]
    if not own:
        scratch += [pltpu.VMEM((slots * tok, HD), jnp.bfloat16)] * 2
    pairs = 10 if own else 22
    out = pl.pallas_call(
        functools.partial(attn_kernel, own, dq_in is not None, final, slots, tok),
        out_shape=[dq_shape] + [jax.ShapeDtypeStruct((2, tok, HD), jnp.bfloat16)] * slots,
        grid_spec=pltpu.PrefetchScalarGridSpec(
            num_scalar_prefetch=1,
            grid=(blocks,),
            in_specs=in_specs,
            out_specs=[dq_spec] + [spec_grad] * slots,
            scratch_shapes=scratch,
        ),
        compiler_params=pltpu.CompilerParams(
            dimension_semantics=("arbitrary",), vmem_limit_bytes=50 << 20),
        cost_estimate=pl.CostEstimate(
            flops=pairs * 10 * KT * ROWS * HD, transcendentals=pairs * KT * ROWS,
            bytes_accessed=10 << 20),
        name="attn_own" if own else "attn_far",
    )(bounds, *args)
    return out[0], list(out[1:])


def block_tables(starts, shard, tok):
    blocks = tok // BQ
    pos = shard * tok + jnp.arange(tok, dtype=jnp.int32)
    begin = jnp.max(jnp.where(starts[None, :] <= pos[:, None], starts[None, :], 0), axis=1)
    begin = (begin - (shard - 2) * tok).reshape(blocks, BQ)
    edge = 2 * tok // KT
    last = edge + jnp.arange(blocks, dtype=jnp.int32) * BQ // KT
    lo = begin[:, 0] // KT
    mid = jnp.minimum((begin[:, -1] + KT - 1) // KT, last)
    far = jnp.stack([jnp.minimum(lo, edge), jnp.minimum(mid, edge), jnp.full_like(lo, edge)])
    near = jnp.stack([jnp.maximum(lo, edge), jnp.maximum(mid, edge), last]) - edge
    beg = jnp.tile(begin, (1, GROUP)).reshape(blocks, 1, ROWS)
    return far.astype(jnp.int32), near.astype(jnp.int32), beg, beg - 2 * tok


def rows_kernel(do_ref, o_ref, lse_ref, delta_ref, lse2_ref):
    heads = lse_ref.shape[0]
    lane = lax.broadcasted_iota(jnp.int32, (1, HD), 1)
    ones = jnp.ones((2 * HD, HD), jnp.bfloat16)
    total = None
    for n in range(heads):
        at = slice(n * HD, (n + 1) * HD)
        prod = do_ref[:, at].astype(jnp.float32) * o_ref[:, at].astype(jnp.float32)
        high = prod.astype(jnp.bfloat16)
        low = (prod - high.astype(jnp.float32)).astype(jnp.bfloat16)
        part = jnp.dot(jnp.concatenate([high, low], axis=1), ones, preferred_element_type=jnp.float32)
        total = part if total is None else jnp.where(lane == n, part, total)
    total = total.T
    for n in range(heads):
        to = slice(n % GROUP * BQ, (n % GROUP + 1) * BQ)
        delta_ref[n // GROUP, 0, :, to] = total[n:n + 1, :]
        lse2_ref[n // GROUP, 0, :, to] = lse_ref[n:n + 1, :] * LOG2E


def row_tables(do, o, lse):
    tok, width = do.shape
    heads = lse.shape[0]
    kv_local = heads // GROUP
    blocks = tok // BQ
    spec = pl.BlockSpec((BQ, width), lambda i: (i, 0))
    spec_row = pl.BlockSpec((kv_local, 1, 1, ROWS), lambda i: (0, i, 0, 0))
    return pl.pallas_call(
        rows_kernel,
        out_shape=[jax.ShapeDtypeStruct((kv_local, blocks, 1, ROWS), jnp.float32)] * 2,
        grid=(blocks,),
        in_specs=[spec, spec, pl.BlockSpec((heads, BQ), lambda i: (0, i))],
        out_specs=[spec_row, spec_row],
        compiler_params=pltpu.CompilerParams(
            dimension_semantics=("arbitrary",), vmem_limit_bytes=58 << 20),
        cost_estimate=pl.CostEstimate(
            flops=4 * tok * width, transcendentals=0, bytes_accessed=4 * tok * width),
        name="row_tables",
    )(do, o, lse)


def ctx_send(array, by):
    n = lax.axis_size("ctx")
    return lax.ppermute(array, "ctx", [(i, i + by) for i in range(n) if 0 <= i + by < n])


def home(array, by):
    n = lax.axis_size("ctx")
    m = lax.axis_size("section")
    pairs = [(s * n + i, (s - 1) % m * n + i - by)
             for s in range(m) for i in range(n) if i - by >= 0]
    return lax.ppermute(array, ("section", "ctx"), pairs)


def tail_kernel(nd, nc, ns, wscale, kv_local, *refs):
    refs = list(refs)
    take = lambda n: [refs.pop(0) for _ in range(n)]
    last = kv_local - 1
    before_parts = [take(3) for _ in range(last)]
    (far2, far1, lse_ref, delta_ref, beg_ref, k_ref, v_ref, q_hbm, do_hbm, dq_hbm, feat_hbm,
     w_ref, vg_ref, kg_ref, dq_ref,
     feat, qv, gv, dqv, qs, dos, pbuf, dqs, dkacc, dvacc, own, landed, back, dvall, dts,
     send, recv, acc, send1, recv1, send2, recv2, acc2,
     lsem, osend, orecv, bsend, brecv, asend, arecv, rsend, rrecv, tsend, trecv, qsend, qrecv) = refs
    z = lax.axis_index("dp")
    c = lax.axis_index("ctx")
    s = lax.axis_index("section")
    scale = HD ** -0.5
    tok = k_ref.shape[0]
    rows = w_ref.shape[0]
    steps = tok // BQ
    cols = slice(last * HD, (last + 1) * HD)
    wide = pl.ds(last * WIDTH, WIDTH)

    loads = [
        pltpu.make_async_copy(src, dst, lsem.at[i])
        for i, (src, dst) in enumerate((
            (q_hbm.at[:, wide], qv), (do_hbm.at[:, wide], gv), (dq_hbm, dqv), (feat_hbm, feat)))]
    for i in (3, 0, 1, 2):
        loads[i].start()

    has_up = z + 1 < nd
    has_down = z >= 1
    to = lax.rem(s + ns - 1, ns)
    come = lax.rem(s + 1, ns)
    barrier = pltpu.get_barrier_semaphore()

    def greet(**device):
        pl.semaphore_signal(barrier, inc=1, device_id=device, device_id_type=MESH)

    col, row = lax.rem(c, 2), c // 2
    across = (row * 2 + 1 - col, (1 - row) * 2 + col)
    for j in range(1, nc):
        greet(ctx=lax.rem(c + j, nc))
    greet(section=come)
    for by in (1, 2):
        @pl.when(c + by < nc)
        def _():
            greet(section=come, ctx=c + by)

    @pl.when(has_up)
    def _():
        greet(dp=z + 1)

    @pl.when(has_down)
    def _():
        greet(dp=z - 1)

    one = lambda cond: jnp.where(cond, 1, 0)
    pl.semaphore_wait(barrier, nc + one(c >= 1) + one(c >= 2) + one(has_up) + one(has_down))

    def hand(src, head, kind):
        return pltpu.make_async_remote_copy(
            src_ref=src.at[kind], dst_ref=landed.at[head, kind],
            send_sem=osend.at[head, kind], recv_sem=orecv.at[head, kind],
            device_id={"section": to}, device_id_type=MESH)

    def partial_home(src, by, kind):
        return pltpu.make_async_remote_copy(
            src_ref=src.at[kind], dst_ref=back.at[by - 1, kind],
            send_sem=bsend.at[by - 1, kind], recv_sem=brecv.at[by - 1, kind],
            device_id={"section": to, "ctx": c - by}, device_id_type=MESH)

    def send_back(kind):
        for by, src in ((2, far2), (1, far1)):
            @pl.when(c >= by)
            def _():
                partial_home(src, by, kind).start()

            @pl.when(c + by >= nc)
            def _():
                back[by - 1, kind] = jnp.zeros((tok, HD), jnp.bfloat16)

    for head in range(last):
        hand(before_parts[head][0], head, 0).start()
    send_back(0)
    for head in range(last):
        hand(before_parts[head][0], head, 1).start()

    def hop(head, src, way, k):
        return pltpu.make_async_remote_copy(
            src_ref=dvall.at[head, src], dst_ref=dvall.at[head, src],
            send_sem=asend.at[head, way, k], recv_sem=arecv.at[head, src],
            device_id={"dp": z + 1 if way == 0 else z - 1}, device_id_type=MESH)

    def each_hop(head, k, act):
        up, down = z - k, z + k

        @pl.when((up >= 0) & has_up)
        def _():
            act(hop(head, up, 0, k))

        @pl.when((down < nd) & has_down)
        def _():
            act(hop(head, down, 1, k))

    def share(j, src):
        return pltpu.make_async_remote_copy(
            src_ref=send.at[j - 1, src], dst_ref=recv.at[j - 1, src],
            send_sem=rsend.at[j - 1, src], recv_sem=rrecv.at[j - 1, src],
            device_id={"ctx": lax.rem(c + j, nc)}, device_id_type=MESH)

    def fold(phase, head, src):
        a, b = ((send1, recv1), (send2, recv2))[phase]
        return pltpu.make_async_remote_copy(
            src_ref=a.at[head, src], dst_ref=b.at[head, src],
            send_sem=tsend.at[phase, head, src], recv_sem=trecv.at[phase, head, src],
            device_id={"ctx": across[phase]}, device_id_type=MESH)

    def product(target):
        return jnp.dot(dts[...], feat[:, pl.ds(pl.multiple_of(target * rows, 128), rows)],
                       preferred_element_type=jnp.float32)

    def process(head, src):
        dts[...] = dvall[head, src].T
        if head == last:
            for j in range(1, nc):
                send[j - 1, src] = product(lax.rem(c + j, nc)).astype(jnp.bfloat16)
                share(j, src).start()
            acc[src] = product(c)
        else:
            for y in (0, 1):
                send1[head, src, y] = product(y * 2 + 1 - col).astype(jnp.bfloat16)
            fold(0, head, src).start()
            for y in (0, 1):
                acc2[head, src, y] = product(y * 2 + col)

    def settle_one(head, src):
        fold(0, head, src).wait_recv()
        away = 1 - row
        send2[head, src] = (acc2[head, src, away] + recv1[head, src, away]).astype(jnp.bfloat16)
        fold(1, head, src).start()

    def settle(head, k):
        if k == 0:
            settle_one(head, z)
        else:
            for src, cond in ((z - k, z >= k), (z + k, z + k < nd)):
                @pl.when(cond)
                def _():
                    settle_one(head, src)

    def weights(head):
        for src in range(nd):
            if head == last:
                total = acc[src]
                for j in range(1, nc):
                    share(j, src).wait_recv()
                    total = total + recv[j - 1, src]
            else:
                fold(1, head, src).wait_recv()
                total = acc2[head, src, row] + recv1[head, src, row] + recv2[head, src]
            at = (src * kv_local + head) * HD
            w_ref[:, at:at + HD] = total.T * wscale

    def advance(head, k):
        up, down = z - k, z + k

        @pl.when(up >= 0)
        def _():
            hop(head, up, 0, 0).wait_recv()

        @pl.when(down < nd)
        def _():
            hop(head, down, 1, 0).wait_recv()

        if k < nd - 1:
            each_hop(head, k, lambda copy: copy.start())

        @pl.when(up >= 0)
        def _():
            process(head, up)

        @pl.when(down < nd)
        def _():
            process(head, down)

    def begin(head, two, one):
        at = slice(head * HD, (head + 1) * HD)
        total = (landed[head, 0].astype(jnp.float32) + two[0] + one[0]).astype(jnp.bfloat16)
        dvall[head, z] = total
        each_hop(head, 0, lambda copy: copy.start())
        vg_ref[:, at] = total

    def send_dq(i):
        at = pl.ds(i * BQ, BQ)
        return pltpu.make_async_remote_copy(
            src_ref=dqs.at[at], dst_ref=dq_ref.at[at], send_sem=qsend.at[i], recv_sem=qrecv.at[i],
            device_id={"section": to}, device_id_type=MESH)

    def stack_rows(i):
        for h in range(GROUP):
            qs[h * BQ:(h + 1) * BQ, :] = qv[i * BQ:(i + 1) * BQ, h * HD:(h + 1) * HD]
            dos[h * BQ:(h + 1) * BQ, :] = gv[i * BQ:(i + 1) * BQ, h * HD:(h + 1) * HD]

    def attend_values(i):
        stack_rows(i)

        def tile(pair, carry):
            start = pl.multiple_of(pair * KT, KT)
            k = k_ref[pl.ds(start, KT), cols]
            sc = lax.dot_general(k, qs[...], (((1,), (1,)), ((), ())), preferred_element_type=jnp.float32)
            p = jnp.exp2(sc * (scale * LOG2E) - lse_ref[last, i])
            u = lax.broadcasted_iota(jnp.int32, (KT, ROWS), 0) + start
            t = (lax.broadcasted_iota(jnp.int32, (1, ROWS), 1) & (BQ - 1)) + i * BQ
            pb = jnp.where((u >= beg_ref[i]) & (u <= t), p, 0.0).astype(jnp.bfloat16)
            pbuf[i * (i + 1) // 2 + pair] = pb
            dvacc[pl.ds(start, KT), :] += jnp.dot(pb, dos[...], preferred_element_type=jnp.float32)
            return carry

        lax.fori_loop(0, i + 1, tile, 0)

    def attend_scores(i):
        stack_rows(i)

        def tile(pair, carry):
            start = pl.multiple_of(pair * KT, KT)
            kt = k_ref[pl.ds(start, KT), cols].T
            v = v_ref[pl.ds(start, KT), cols]
            p = pbuf[i * (i + 1) // 2 + pair].astype(jnp.float32)
            dp = lax.dot_general(v, dos[...], (((1,), (1,)), ((), ())), preferred_element_type=jnp.float32)
            ds = (p * (dp - delta_ref[last, i])).astype(jnp.bfloat16)
            dkacc[pl.ds(start, KT), :] += jnp.dot(ds, qs[...], preferred_element_type=jnp.float32)
            dqv[i] += jnp.dot(kt, ds, preferred_element_type=jnp.float32)
            return carry

        lax.fori_loop(0, i + 1, tile, 0)
        for h in range(GROUP):
            dqs[i * BQ:(i + 1) * BQ, h * HD:(h + 1) * HD] = (
                dqv[i, :, h * BQ:(h + 1) * BQ].T * scale).astype(jnp.bfloat16)
        send_dq(i).start()

    dkacc[...] = jnp.zeros_like(dkacc)
    dvacc[...] = jnp.zeros_like(dvacc)
    for head in range(last):
        hand(before_parts[head][0], head, 0).wait_recv()
        begin(head, before_parts[head][1], before_parts[head][2])
    loads[3].wait()
    for head in range(last):
        process(head, z)
    loads[0].wait()
    loads[1].wait()
    for i in reversed(range(steps)):
        attend_values(i)
        for head in range(last):
            if i == steps - 1:
                advance(head, 1)
            if i == steps - 2:
                settle(head, 0)
    send_back(1)
    own[0] = dvacc[...].astype(jnp.bfloat16)
    hand(own, last, 0).start()
    for by in (2, 1):
        @pl.when(c + by < nc)
        def _():
            partial_home(far1, by, 0).wait_recv()
    hand(own, last, 0).wait_recv()
    begin(last, back.at[1], back.at[0])
    process(last, z)
    loads[2].wait()
    todo = []
    for k in range(2, nd):
        for head in range(last):
            todo += [(advance, head, k), (settle, head, k - 1)]
        if k < nd - 1:
            todo += [(advance, last, k - 1)]
    todo += [(advance, last, nd - 2)]
    todo += [(settle, head, nd - 1) for head in range(last)]

    def run(n):
        for act, head, k in todo[:n]:
            act(head, k)
        del todo[:n]

    for i in reversed(range(steps)):
        attend_scores(i)
        if i == 0:
            own[1] = (dkacc[...] * scale).astype(jnp.bfloat16)
            hand(own, last, 1).start()
        run(2 if i == steps - 1 else 1)
    run(len(todo))
    for head in range(last):
        weights(head)
    for head in range(kv_local):
        if head == last:
            for by in (2, 1):
                @pl.when(c + by < nc)
                def _():
                    partial_home(far1, by, 1).wait_recv()
            two, one_ref = back.at[1], back.at[0]
            hand(own, head, 1).wait_recv()
        else:
            two, one_ref = before_parts[head][1:]
            hand(before_parts[head][0], head, 1).wait_recv()
        kg_ref[:, head * HD:(head + 1) * HD] = (
            landed[head, 1].astype(jnp.float32) + two[1] + one_ref[1]).astype(jnp.bfloat16)
    advance(last, nd - 1)
    for head in range(kv_local):
        for kind in (0, 1):
            hand(own if head == last else before_parts[head][0], head, kind).wait_send()
        for k in range(nd - 1):
            each_hop(head, k, lambda copy: copy.wait_send())
    for kind in (0, 1):
        for by, src in ((2, far2), (1, far1)):
            @pl.when(c >= by)
            def _():
                partial_home(src, by, kind).wait_send()
    for i in range(steps):
        send_dq(i).wait()
    weights(last)

    def drain(i, carry):
        for j in range(1, nc):
            share(j, i).wait_send()
        for head in range(last):
            for phase in (0, 1):
                fold(phase, head, i).wait_send()
        return carry

    lax.fori_loop(0, nd, drain, 0)


def tail(feat, q, do, k, v, lse, delta, beg, parts, far, dq, nd, nc, ns, scale):
    tok, width = feat.shape
    rows = width // nc
    kv_local = len(parts) + 1
    others = max(len(parts), 1)
    steps = tok // BQ
    bf16, f32 = jnp.bfloat16, jnp.float32
    vmem, dma = pltpu.VMEM, pltpu.SemaphoreType.DMA
    whole = pl.BlockSpec(memory_space=pltpu.VMEM)
    return pl.pallas_call(
        functools.partial(tail_kernel, nd, nc, ns, scale, kv_local),
        out_shape=[
            jax.ShapeDtypeStruct((rows, nd * kv_local * HD), f32),
            jax.ShapeDtypeStruct((tok, kv_local * HD), bf16),
            jax.ShapeDtypeStruct((tok, kv_local * HD), bf16),
            jax.ShapeDtypeStruct((tok, WIDTH), bf16),
        ],
        in_specs=[whole] * (3 * len(parts) + 7) + [pl.BlockSpec(memory_space=pl.ANY)] * 4,
        out_specs=[whole] * 3 + [pl.BlockSpec(memory_space=pl.ANY)],
        scratch_shapes=[
            vmem((tok, width), bf16),
            vmem((tok, WIDTH), bf16),
            vmem((tok, WIDTH), bf16),
            vmem((steps, HD, ROWS), f32),
            vmem((ROWS, HD), bf16),
            vmem((ROWS, HD), bf16),
            vmem((steps * (steps + 1) // 2, KT, ROWS), bf16),
            vmem((tok, WIDTH), bf16),
            vmem((tok, HD), f32),
            vmem((tok, HD), f32),
            vmem((2, tok, HD), bf16),
            vmem((kv_local, 2, tok, HD), bf16),
            vmem((2, 2, tok, HD), bf16),
            vmem((kv_local, nd, tok, HD), bf16),
            vmem((HD, tok), bf16),
            vmem((nc - 1, nd, HD, rows), bf16),
            vmem((nc - 1, nd, HD, rows), bf16),
            vmem((nd, HD, rows), f32),
            vmem((others, nd, 2, HD, rows), bf16),
            vmem((others, nd, 2, HD, rows), bf16),
            vmem((others, nd, HD, rows), bf16),
            vmem((others, nd, HD, rows), bf16),
            vmem((others, nd, 2, HD, rows), f32),
            dma((4,)),
            dma((kv_local, 2)),
            dma((kv_local, 2)),
            dma((2, 2)),
            dma((2, 2)),
            dma((kv_local, 2, nd)),
            dma((kv_local, nd)),
            dma((nc - 1, nd)),
            dma((nc - 1, nd)),
            dma((2, others, nd)),
            dma((2, others, nd)),
            dma((steps,)),
            dma((steps,)),
        ],
        compiler_params=pltpu.CompilerParams(
            collective_id=0, has_side_effects=True, vmem_limit_bytes=62 << 20),
        cost_estimate=pl.CostEstimate(
            flops=2 * tok * width * nd * kv_local * HD + 10 * 10 * KT * ROWS * HD,
            transcendentals=10 * KT * ROWS, bytes_accessed=20 << 20),
        name="tail",
    )(*[part for head in parts for part in head], *far, lse, delta, beg, k, v, q, do, dq, feat)


def finish_kernel(*refs):
    *parts, weight, value, key, dq_out, w_out, v_out, k_out = refs
    width = parts[0].shape[2]
    for i, part in enumerate(parts):
        dq_out[:, :, i * width:(i + 1) * width] = part[...]
    w_out[0] = weight[...]
    v_out[0] = value[...]
    k_out[0] = key[...]


def finish(dq_parts, weight, value, key):
    _, tok, width = dq_parts[0].shape
    n = 4
    cut = lambda a: pl.BlockSpec((a.shape[0] // n, a.shape[1]), lambda i: (i, 0))
    cut3 = lambda a: pl.BlockSpec((1, a.shape[0] // n, a.shape[1]), lambda i: (0, i, 0))
    wide = lambda w: pl.BlockSpec((1, tok // n, w), lambda i: (0, i, 0))
    return pl.pallas_call(
        finish_kernel,
        out_shape=[
            jax.ShapeDtypeStruct((1, tok, width * len(dq_parts)), jnp.bfloat16),
            jax.ShapeDtypeStruct((1, *weight.shape), weight.dtype),
            jax.ShapeDtypeStruct((1, *value.shape), value.dtype),
            jax.ShapeDtypeStruct((1, *key.shape), key.dtype),
        ],
        grid=(n,),
        in_specs=[wide(width)] * len(dq_parts) + [cut(weight), cut(value), cut(key)],
        out_specs=[wide(width * len(dq_parts)), cut3(weight), cut3(value), cut3(key)],
        compiler_params=pltpu.CompilerParams(
            dimension_semantics=("arbitrary",), vmem_limit_bytes=60 << 20),
        name="finish",
    )(*dq_parts, weight, value, key)


def weight_plain(feat, dv, nd, nc, scale):
    shard = lax.axis_index("ctx")
    rows = feat.shape[1] // nc
    dv_all = lax.all_gather(dv, "dp", axis=1, tiled=True)

    def partial(target):
        cols = lax.dynamic_slice_in_dim(feat, target * rows, rows, 1)
        return lax.dot_general(cols, dv_all, (((0,), (0,)), ((), ())),
                               preferred_element_type=jnp.float32)

    total = partial(shard)
    for by in range(1, nc):
        sent = partial((shard + by) % nc).astype(jnp.bfloat16)
        total = total + lax.ppermute(sent, "ctx", [(i, (i + by) % nc) for i in range(nc)])
    return total * scale


def local(features, queries, keys, values, attn_out, out_grad, lse, doc_starts, key_blocks):
    tok = queries.shape[1]
    kv_local = keys.shape[2] // HD
    shard = lax.axis_index("ctx")
    nc = lax.axis_size("ctx")
    nd = lax.axis_size("dp")
    ns = lax.axis_size("section")
    q, do, k, v = queries[0], out_grad[0], keys[0], values[0]

    def window(head):
        return ctx_send(packed[head], 2), ctx_send(packed[head], 1)

    packed = [jnp.concatenate([k[:, head * HD:(head + 1) * HD], v[:, head * HD:(head + 1) * HD]], axis=1)
              for head in range(kv_local)]
    windows = [window(0)]
    far, near, beg_far, beg_near = block_tables(doc_starts[0], shard, tok)
    delta, lse2 = row_tables(do, attn_out[0], lse[0])
    scale = (tok * nc) ** -0.5
    feat = features[0]
    last = kv_local - 1
    dq_parts, parts = [], []
    for head in range(last):
        dq, (own,) = attention(head, True, near, q, do, lse2, delta, beg_near, (k, v), None, False)
        packed[head + 1], _ = lax.optimization_barrier((packed[head + 1], own))
        windows.append(window(head + 1))
        dq, (two, one) = attention(head, False, far, q, do, lse2, delta, beg_far, windows[head], dq, True)
        far, _ = lax.optimization_barrier((far, two))
        dq_parts.append(home(dq, 0))
        parts.append((own, home(two, 2), home(one, 1)))
    dq, (two, one) = attention(last, False, far, q, do, lse2, delta, beg_far, windows[last], None, False)
    if nc == 4 and feat.shape[1] // nc % 128 == 0:
        weight, value_grad, key_grad, dq = tail(
            feat, q, do, k, v, lse2, delta, beg_near, parts, (two, one), dq, nd, nc, ns, scale)
        dq_parts.append(dq[None])
        query_grad, weight, value_grad, key_grad = finish(dq_parts, weight, value_grad, key_grad)
        return query_grad, key_grad, value_grad, weight
    else:
        dq, (own,) = attention(last, True, near, q, do, lse2, delta, beg_near, (k, v), dq, True)
        dq_parts.append(home(dq, 0))
        parts.append((own, home(two, 2), home(one, 1)))
        grads = [(home(own, 0).astype(jnp.float32) + two + one).astype(jnp.bfloat16) for own, two, one in parts]
        value_grad = jnp.concatenate([grad[0] for grad in grads], axis=1)
        key_grad = jnp.concatenate([grad[1] for grad in grads], axis=1)
        weight = weight_plain(feat, value_grad, nd, nc, scale)
    query_grad = jnp.concatenate(dq_parts, axis=2)
    return query_grad, key_grad[None], value_grad[None], weight[None]


def solution(mesh):
    placed = (
        P("section", "ctx", "dp"),
        P("section", "ctx", "dp"),
        P("section", "ctx", "dp"),
        P("section", "ctx", "dp"),
        P("section", "ctx", "dp"),
        P("section", "ctx", "dp"),
        P("section", "dp", "ctx"),
        P("section", None),
        P("section", "ctx", None),
    )
    return jax.shard_map(
        local,
        mesh=mesh,
        in_specs=placed,
        out_specs=(
            P("section", "ctx", "dp"),
            P("section", "ctx", "dp"),
            P("section", "ctx", "dp"),
            P("section", ("dp", "ctx"), None),
        ),
        check_vma=False,
    )
```

```python
import functools

import jax
import jax.numpy as jnp
from jax import lax
from jax.experimental import pallas as pl
from jax.experimental.pallas import tpu as pltpu
from jax.sharding import PartitionSpec as P

QH = 64
KVH = 8
HD = 128
GROUP = QH // KVH
LOG2E = 1.4426950408889634
KT = 256
BQ = 256
ROWS = GROUP * BQ
WIDTH = GROUP * HD
MESH = pl.DeviceIdType.MESH


def attn_kernel(own, resume, final, slots, tok, *refs):
    refs = list(refs)
    bounds = refs.pop(0)
    q_ref, do_ref, lse_ref, delta_ref, beg_ref = (refs.pop(0) for _ in range(5))
    if own:
        k_ref, v_ref = refs.pop(0), refs.pop(0)
    else:
        kv_refs = [refs.pop(0) for _ in range(slots)]
    dq_in = refs.pop(0) if resume else None
    dq_ref = refs.pop(0)
    grads = [refs.pop(0) for _ in range(slots)]
    dkacc, dvacc, qs, dos, dqacc = (refs.pop(0) for _ in range(5))
    if not own:
        k_ref, v_ref = refs.pop(0), refs.pop(0)

    step = pl.program_id(0)
    scale = HD ** -0.5
    base = 0 if own else slots * tok
    row0 = base + step * BQ

    @pl.when(step == 0)
    def _():
        if not own:
            for slot, ref in enumerate(kv_refs):
                k_ref[slot * tok:(slot + 1) * tok, :] = ref[:, :HD]
                v_ref[slot * tok:(slot + 1) * tok, :] = ref[:, HD:]
        dkacc[...] = jnp.zeros_like(dkacc)
        dvacc[...] = jnp.zeros_like(dvacc)

    for h in range(GROUP):
        qs[h * BQ:(h + 1) * BQ, :] = q_ref[:, h * HD:(h + 1) * HD]
        dos[h * BQ:(h + 1) * BQ, :] = do_ref[:, h * HD:(h + 1) * HD]
    dqacc[...] = dq_in[0] if resume else jnp.zeros_like(dqacc)

    def tile(pair, masked):
        start = pl.multiple_of(pair * KT, KT)
        k = k_ref[pl.ds(start, KT), :]
        kt = k.T
        v = v_ref[pl.ds(start, KT), :]
        q = qs[...]
        g = dos[...]
        s = lax.dot_general(k, q, (((1,), (1,)), ((), ())), preferred_element_type=jnp.float32)
        p = jnp.exp2(s * (scale * LOG2E) - lse_ref[0, 0])
        if masked:
            u = lax.broadcasted_iota(jnp.int32, (KT, ROWS), 0) + start
            allowed = u >= beg_ref[0]
            if own:
                t = (lax.broadcasted_iota(jnp.int32, (1, ROWS), 1) & (BQ - 1)) + row0
                allowed &= u <= t
            p = jnp.where(allowed, p, 0.0)
        dp = lax.dot_general(v, g, (((1,), (1,)), ((), ())), preferred_element_type=jnp.float32)
        ds = (p * (dp - delta_ref[0, 0])).astype(jnp.bfloat16)
        pb = p.astype(jnp.bfloat16)
        dvacc[pl.ds(start, KT), :] += jnp.dot(pb, g, preferred_element_type=jnp.float32)
        dkacc[pl.ds(start, KT), :] += jnp.dot(ds, q, preferred_element_type=jnp.float32)
        dqacc[...] += jnp.dot(kt, ds, preferred_element_type=jnp.float32)

    lo = bounds[0, step]
    mid = bounds[1, step]
    last = bounds[2, step]
    edge = mid - lo

    def masked_step(i, carry):
        tile(jnp.where(i < edge, lo + i, last), True)
        return carry

    def plain_step(i, carry):
        tile(i, False)
        return carry

    lax.fori_loop(0, edge + 1 if own else edge, masked_step, 0)
    lax.fori_loop(mid, last, plain_step, 0)

    if final:
        for h in range(GROUP):
            dq_ref[0, :, h * HD:(h + 1) * HD] = (dqacc[:, h * BQ:(h + 1) * BQ].T * scale).astype(jnp.bfloat16)
    else:
        dq_ref[0] = dqacc[...]

    @pl.when(step == pl.num_programs(0) - 1)
    def _():
        for slot, ref in enumerate(grads):
            at = slice(slot * tok, (slot + 1) * tok)
            ref[0] = dvacc[at, :].astype(jnp.bfloat16)
            ref[1] = (dkacc[at, :] * scale).astype(jnp.bfloat16)


def attention(head, own, bounds, q, do, lse, delta, beg, kv, dq_in, final):
    tok, width = q.shape
    blocks = tok // BQ
    slots = 1 if own else 2
    spec_q = pl.BlockSpec((BQ, WIDTH), lambda i, *_: (i, head))
    spec_row = pl.BlockSpec((1, 1, 1, ROWS), lambda i, *_: (head, i, 0, 0))
    spec_acc = pl.BlockSpec((1, HD, ROWS), lambda i, *_: (i, 0, 0))
    spec_grad = pl.BlockSpec((2, tok, HD), lambda i, *_: (0, 0, 0))
    in_specs = [spec_q, spec_q, spec_row, spec_row, pl.BlockSpec((1, 1, ROWS), lambda i, *_: (i, 0, 0))]
    args = [q, do, lse, delta, beg]
    if own:
        in_specs += [pl.BlockSpec((tok, HD), lambda i, *_: (0, head))] * 2
    else:
        in_specs += [pl.BlockSpec((tok, 2 * HD), lambda i, *_: (0, 0))] * 2
    args += list(kv)
    if dq_in is not None:
        in_specs.append(spec_acc)
        args.append(dq_in)
    if final:
        dq_shape = jax.ShapeDtypeStruct((1, tok, WIDTH), jnp.bfloat16)
        dq_spec = pl.BlockSpec((1, BQ, WIDTH), lambda i, *_: (0, i, 0))
    else:
        dq_shape, dq_spec = jax.ShapeDtypeStruct((blocks, HD, ROWS), jnp.float32), spec_acc
    scratch = [
        pltpu.VMEM((slots * tok, HD), jnp.float32),
        pltpu.VMEM((slots * tok, HD), jnp.float32),
        pltpu.VMEM((ROWS, HD), jnp.bfloat16),
        pltpu.VMEM((ROWS, HD), jnp.bfloat16),
        pltpu.VMEM((HD, ROWS), jnp.float32),
    ]
    if not own:
        scratch += [pltpu.VMEM((slots * tok, HD), jnp.bfloat16)] * 2
    pairs = 10 if own else 22
    out = pl.pallas_call(
        functools.partial(attn_kernel, own, dq_in is not None, final, slots, tok),
        out_shape=[dq_shape] + [jax.ShapeDtypeStruct((2, tok, HD), jnp.bfloat16)] * slots,
        grid_spec=pltpu.PrefetchScalarGridSpec(
            num_scalar_prefetch=1,
            grid=(blocks,),
            in_specs=in_specs,
            out_specs=[dq_spec] + [spec_grad] * slots,
            scratch_shapes=scratch,
        ),
        compiler_params=pltpu.CompilerParams(
            dimension_semantics=("arbitrary",), vmem_limit_bytes=50 << 20),
        cost_estimate=pl.CostEstimate(
            flops=pairs * 10 * KT * ROWS * HD, transcendentals=pairs * KT * ROWS,
            bytes_accessed=10 << 20),
        name="attn_own" if own else "attn_far",
    )(bounds, *args)
    return out[0], list(out[1:])


def block_tables(starts, shard, tok):
    blocks = tok // BQ
    pos = shard * tok + jnp.arange(tok, dtype=jnp.int32)
    begin = jnp.max(jnp.where(starts[None, :] <= pos[:, None], starts[None, :], 0), axis=1)
    begin = (begin - (shard - 2) * tok).reshape(blocks, BQ)
    edge = 2 * tok // KT
    last = edge + jnp.arange(blocks, dtype=jnp.int32) * BQ // KT
    lo = begin[:, 0] // KT
    mid = jnp.minimum((begin[:, -1] + KT - 1) // KT, last)
    far = jnp.stack([jnp.minimum(lo, edge), jnp.minimum(mid, edge), jnp.full_like(lo, edge)])
    near = jnp.stack([jnp.maximum(lo, edge), jnp.maximum(mid, edge), last]) - edge
    beg = jnp.tile(begin, (1, GROUP)).reshape(blocks, 1, ROWS)
    return far.astype(jnp.int32), near.astype(jnp.int32), beg, beg - 2 * tok


def rows_kernel(do_ref, o_ref, lse_ref, delta_ref, lse2_ref):
    heads = lse_ref.shape[0]
    lane = lax.broadcasted_iota(jnp.int32, (1, HD), 1)
    ones = jnp.ones((2 * HD, HD), jnp.bfloat16)
    total = None
    for n in range(heads):
        at = slice(n * HD, (n + 1) * HD)
        prod = do_ref[:, at].astype(jnp.float32) * o_ref[:, at].astype(jnp.float32)
        high = prod.astype(jnp.bfloat16)
        low = (prod - high.astype(jnp.float32)).astype(jnp.bfloat16)
        part = jnp.dot(jnp.concatenate([high, low], axis=1), ones, preferred_element_type=jnp.float32)
        total = part if total is None else jnp.where(lane == n, part, total)
    total = total.T
    for n in range(heads):
        to = slice(n % GROUP * BQ, (n % GROUP + 1) * BQ)
        delta_ref[n // GROUP, 0, :, to] = total[n:n + 1, :]
        lse2_ref[n // GROUP, 0, :, to] = lse_ref[n:n + 1, :] * LOG2E


def row_tables(do, o, lse):
    tok, width = do.shape
    heads = lse.shape[0]
    kv_local = heads // GROUP
    blocks = tok // BQ
    spec = pl.BlockSpec((BQ, width), lambda i: (i, 0))
    spec_row = pl.BlockSpec((kv_local, 1, 1, ROWS), lambda i: (0, i, 0, 0))
    return pl.pallas_call(
        rows_kernel,
        out_shape=[jax.ShapeDtypeStruct((kv_local, blocks, 1, ROWS), jnp.float32)] * 2,
        grid=(blocks,),
        in_specs=[spec, spec, pl.BlockSpec((heads, BQ), lambda i: (0, i))],
        out_specs=[spec_row, spec_row],
        compiler_params=pltpu.CompilerParams(
            dimension_semantics=("arbitrary",), vmem_limit_bytes=58 << 20),
        cost_estimate=pl.CostEstimate(
            flops=4 * tok * width, transcendentals=0, bytes_accessed=4 * tok * width),
        name="row_tables",
    )(do, o, lse)


def ctx_send(array, by):
    n = lax.axis_size("ctx")
    return lax.ppermute(array, "ctx", [(i, i + by) for i in range(n) if 0 <= i + by < n])


def home(array, by):
    n = lax.axis_size("ctx")
    m = lax.axis_size("section")
    pairs = [(s * n + i, (s - 1) % m * n + i - by)
             for s in range(m) for i in range(n) if i - by >= 0]
    return lax.ppermute(array, ("section", "ctx"), pairs)


def tail_kernel(nd, nc, ns, wscale, kv_local, *refs):
    refs = list(refs)
    take = lambda n: [refs.pop(0) for _ in range(n)]
    last = kv_local - 1
    before_parts = [take(3) for _ in range(last)]
    (far2, far1, lse_ref, delta_ref, beg_ref, k_ref, v_ref, q_hbm, do_hbm, dq_hbm, feat_hbm,
     w_ref, vg_ref, kg_ref, dq_ref,
     feat, qv, gv, dqv, qs, dos, pbuf, dqs, dkacc, dvacc, own, landed, back, dvall, dts,
     send, recv, acc, send1, recv1, send2, recv2, acc2,
     lsem, osend, orecv, bsend, brecv, asend, arecv, rsend, rrecv, tsend, trecv, qsend, qrecv) = refs
    z = lax.axis_index("dp")
    c = lax.axis_index("ctx")
    s = lax.axis_index("section")
    scale = HD ** -0.5
    tok = k_ref.shape[0]
    rows = w_ref.shape[0]
    steps = tok // BQ
    cols = slice(last * HD, (last + 1) * HD)
    wide = pl.ds(last * WIDTH, WIDTH)

    loads = [
        pltpu.make_async_copy(src, dst, lsem.at[i])
        for i, (src, dst) in enumerate((
            (q_hbm.at[:, wide], qv), (do_hbm.at[:, wide], gv), (dq_hbm, dqv), (feat_hbm, feat)))]
    for i in (3, 0, 1, 2):
        loads[i].start()

    has_up = z + 1 < nd
    has_down = z >= 1
    to = lax.rem(s + ns - 1, ns)
    come = lax.rem(s + 1, ns)
    barrier = pltpu.get_barrier_semaphore()

    def greet(**device):
        pl.semaphore_signal(barrier, inc=1, device_id=device, device_id_type=MESH)

    col, row = lax.rem(c, 2), c // 2
    across = (row * 2 + 1 - col, (1 - row) * 2 + col)
    for j in range(1, nc):
        greet(ctx=lax.rem(c + j, nc))
    greet(section=come)
    for by in (1, 2):
        @pl.when(c + by < nc)
        def _():
            greet(section=come, ctx=c + by)

    @pl.when(has_up)
    def _():
        greet(dp=z + 1)

    @pl.when(has_down)
    def _():
        greet(dp=z - 1)

    one = lambda cond: jnp.where(cond, 1, 0)
    pl.semaphore_wait(barrier, nc + one(c >= 1) + one(c >= 2) + one(has_up) + one(has_down))

    def hand(src, head, kind):
        return pltpu.make_async_remote_copy(
            src_ref=src.at[kind], dst_ref=landed.at[head, kind],
            send_sem=osend.at[head, kind], recv_sem=orecv.at[head, kind],
            device_id={"section": to}, device_id_type=MESH)

    def partial_home(src, by, kind):
        return pltpu.make_async_remote_copy(
            src_ref=src.at[kind], dst_ref=back.at[by - 1, kind],
            send_sem=bsend.at[by - 1, kind], recv_sem=brecv.at[by - 1, kind],
            device_id={"section": to, "ctx": c - by}, device_id_type=MESH)

    def send_back(kind):
        for by, src in ((2, far2), (1, far1)):
            @pl.when(c >= by)
            def _():
                partial_home(src, by, kind).start()

            @pl.when(c + by >= nc)
            def _():
                back[by - 1, kind] = jnp.zeros((tok, HD), jnp.bfloat16)

    for head in range(last):
        hand(before_parts[head][0], head, 0).start()
    send_back(0)
    for head in range(last):
        hand(before_parts[head][0], head, 1).start()

    def hop(head, src, way, k):
        return pltpu.make_async_remote_copy(
            src_ref=dvall.at[head, src], dst_ref=dvall.at[head, src],
            send_sem=asend.at[head, way, k], recv_sem=arecv.at[head, src],
            device_id={"dp": z + 1 if way == 0 else z - 1}, device_id_type=MESH)

    def each_hop(head, k, act):
        up, down = z - k, z + k

        @pl.when((up >= 0) & has_up)
        def _():
            act(hop(head, up, 0, k))

        @pl.when((down < nd) & has_down)
        def _():
            act(hop(head, down, 1, k))

    def share(j, src):
        return pltpu.make_async_remote_copy(
            src_ref=send.at[j - 1, src], dst_ref=recv.at[j - 1, src],
            send_sem=rsend.at[j - 1, src], recv_sem=rrecv.at[j - 1, src],
            device_id={"ctx": lax.rem(c + j, nc)}, device_id_type=MESH)

    def fold(phase, head, src):
        a, b = ((send1, recv1), (send2, recv2))[phase]
        return pltpu.make_async_remote_copy(
            src_ref=a.at[head, src], dst_ref=b.at[head, src],
            send_sem=tsend.at[phase, head, src], recv_sem=trecv.at[phase, head, src],
            device_id={"ctx": across[phase]}, device_id_type=MESH)

    def product(target):
        return jnp.dot(dts[...], feat[:, pl.ds(pl.multiple_of(target * rows, 128), rows)],
                       preferred_element_type=jnp.float32)

    def process(head, src):
        dts[...] = dvall[head, src].T
        if head == last:
            for j in range(1, nc):
                send[j - 1, src] = product(lax.rem(c + j, nc)).astype(jnp.bfloat16)
                share(j, src).start()
            acc[src] = product(c)
        else:
            for y in (0, 1):
                send1[head, src, y] = product(y * 2 + 1 - col).astype(jnp.bfloat16)
            fold(0, head, src).start()
            for y in (0, 1):
                acc2[head, src, y] = product(y * 2 + col)

    def settle_one(head, src):
        fold(0, head, src).wait_recv()
        away = 1 - row
        send2[head, src] = (acc2[head, src, away] + recv1[head, src, away]).astype(jnp.bfloat16)
        fold(1, head, src).start()

    def settle(head, k):
        if k == 0:
            settle_one(head, z)
        else:
            for src, cond in ((z - k, z >= k), (z + k, z + k < nd)):
                @pl.when(cond)
                def _():
                    settle_one(head, src)

    def weights(head):
        for src in range(nd):
            if head == last:
                total = acc[src]
                for j in range(1, nc):
                    share(j, src).wait_recv()
                    total = total + recv[j - 1, src]
            else:
                fold(1, head, src).wait_recv()
                total = acc2[head, src, row] + recv1[head, src, row] + recv2[head, src]
            at = (src * kv_local + head) * HD
            w_ref[:, at:at + HD] = total.T * wscale

    def advance(head, k):
        up, down = z - k, z + k

        @pl.when(up >= 0)
        def _():
            hop(head, up, 0, 0).wait_recv()

        @pl.when(down < nd)
        def _():
            hop(head, down, 1, 0).wait_recv()

        if k < nd - 1:
            each_hop(head, k, lambda copy: copy.start())

        @pl.when(up >= 0)
        def _():
            process(head, up)

        @pl.when(down < nd)
        def _():
            process(head, down)

    def begin(head, two, one):
        at = slice(head * HD, (head + 1) * HD)
        total = (landed[head, 0].astype(jnp.float32) + two[0] + one[0]).astype(jnp.bfloat16)
        dvall[head, z] = total
        each_hop(head, 0, lambda copy: copy.start())
        vg_ref[:, at] = total

    def send_dq(i):
        at = pl.ds(i * BQ, BQ)
        return pltpu.make_async_remote_copy(
            src_ref=dqs.at[at], dst_ref=dq_ref.at[at], send_sem=qsend.at[i], recv_sem=qrecv.at[i],
            device_id={"section": to}, device_id_type=MESH)

    def stack_rows(i):
        for h in range(GROUP):
            qs[h * BQ:(h + 1) * BQ, :] = qv[i * BQ:(i + 1) * BQ, h * HD:(h + 1) * HD]
            dos[h * BQ:(h + 1) * BQ, :] = gv[i * BQ:(i + 1) * BQ, h * HD:(h + 1) * HD]

    def attend_values(i):
        stack_rows(i)

        def tile(pair, carry):
            start = pl.multiple_of(pair * KT, KT)
            k = k_ref[pl.ds(start, KT), cols]
            sc = lax.dot_general(k, qs[...], (((1,), (1,)), ((), ())), preferred_element_type=jnp.float32)
            p = jnp.exp2(sc * (scale * LOG2E) - lse_ref[last, i])
            u = lax.broadcasted_iota(jnp.int32, (KT, ROWS), 0) + start
            t = (lax.broadcasted_iota(jnp.int32, (1, ROWS), 1) & (BQ - 1)) + i * BQ
            pb = jnp.where((u >= beg_ref[i]) & (u <= t), p, 0.0).astype(jnp.bfloat16)
            pbuf[i * (i + 1) // 2 + pair] = pb
            dvacc[pl.ds(start, KT), :] += jnp.dot(pb, dos[...], preferred_element_type=jnp.float32)
            return carry

        lax.fori_loop(0, i + 1, tile, 0)

    def attend_scores(i):
        stack_rows(i)

        def tile(pair, carry):
            start = pl.multiple_of(pair * KT, KT)
            kt = k_ref[pl.ds(start, KT), cols].T
            v = v_ref[pl.ds(start, KT), cols]
            p = pbuf[i * (i + 1) // 2 + pair].astype(jnp.float32)
            dp = lax.dot_general(v, dos[...], (((1,), (1,)), ((), ())), preferred_element_type=jnp.float32)
            ds = (p * (dp - delta_ref[last, i])).astype(jnp.bfloat16)
            dkacc[pl.ds(start, KT), :] += jnp.dot(ds, qs[...], preferred_element_type=jnp.float32)
            dqv[i] += jnp.dot(kt, ds, preferred_element_type=jnp.float32)
            return carry

        lax.fori_loop(0, i + 1, tile, 0)
        for h in range(GROUP):
            dqs[i * BQ:(i + 1) * BQ, h * HD:(h + 1) * HD] = (
                dqv[i, :, h * BQ:(h + 1) * BQ].T * scale).astype(jnp.bfloat16)
        send_dq(i).start()

    dkacc[...] = jnp.zeros_like(dkacc)
    dvacc[...] = jnp.zeros_like(dvacc)
    for head in range(last):
        hand(before_parts[head][0], head, 0).wait_recv()
        begin(head, before_parts[head][1], before_parts[head][2])
    loads[3].wait()
    for head in range(last):
        process(head, z)
    loads[0].wait()
    loads[1].wait()
    for i in reversed(range(steps)):
        attend_values(i)
        for head in range(last):
            if i == steps - 1:
                advance(head, 1)
            if i == steps - 2:
                settle(head, 0)
    send_back(1)
    own[0] = dvacc[...].astype(jnp.bfloat16)
    hand(own, last, 0).start()
    for by in (2, 1):
        @pl.when(c + by < nc)
        def _():
            partial_home(far1, by, 0).wait_recv()
    hand(own, last, 0).wait_recv()
    begin(last, back.at[1], back.at[0])
    process(last, z)
    loads[2].wait()
    todo = []
    for k in range(2, nd):
        for head in range(last):
            todo += [(advance, head, k), (settle, head, k - 1)]
        if k < nd - 1:
            todo += [(advance, last, k - 1)]
    todo += [(advance, last, nd - 2)]
    todo += [(settle, head, nd - 1) for head in range(last)]

    def run(n):
        for act, head, k in todo[:n]:
            act(head, k)
        del todo[:n]

    for i in reversed(range(steps)):
        attend_scores(i)
        if i == 0:
            own[1] = (dkacc[...] * scale).astype(jnp.bfloat16)
            hand(own, last, 1).start()
        run(2 if i == steps - 1 else 1)
    run(len(todo))
    for head in range(last):
        weights(head)
    for head in range(kv_local):
        if head == last:
            for by in (2, 1):
                @pl.when(c + by < nc)
                def _():
                    partial_home(far1, by, 1).wait_recv()
            two, one_ref = back.at[1], back.at[0]
            hand(own, head, 1).wait_recv()
        else:
            two, one_ref = before_parts[head][1:]
            hand(before_parts[head][0], head, 1).wait_recv()
        kg_ref[:, head * HD:(head + 1) * HD] = (
            landed[head, 1].astype(jnp.float32) + two[1] + one_ref[1]).astype(jnp.bfloat16)
    advance(last, nd - 1)
    for head in range(kv_local):
        for kind in (0, 1):
            hand(own if head == last else before_parts[head][0], head, kind).wait_send()
        for k in range(nd - 1):
            each_hop(head, k, lambda copy: copy.wait_send())
    for kind in (0, 1):
        for by, src in ((2, far2), (1, far1)):
            @pl.when(c >= by)
            def _():
                partial_home(src, by, kind).wait_send()
    for i in range(steps):
        send_dq(i).wait()
    weights(last)

    def drain(i, carry):
        for j in range(1, nc):
            share(j, i).wait_send()
        for head in range(last):
            for phase in (0, 1):
                fold(phase, head, i).wait_send()
        return carry

    lax.fori_loop(0, nd, drain, 0)


def tail(feat, q, do, k, v, lse, delta, beg, parts, far, dq, nd, nc, ns, scale):
    tok, width = feat.shape
    rows = width // nc
    kv_local = len(parts) + 1
    others = max(len(parts), 1)
    steps = tok // BQ
    bf16, f32 = jnp.bfloat16, jnp.float32
    vmem, dma = pltpu.VMEM, pltpu.SemaphoreType.DMA
    whole = pl.BlockSpec(memory_space=pltpu.VMEM)
    return pl.pallas_call(
        functools.partial(tail_kernel, nd, nc, ns, scale, kv_local),
        out_shape=[
            jax.ShapeDtypeStruct((rows, nd * kv_local * HD), f32),
            jax.ShapeDtypeStruct((tok, kv_local * HD), bf16),
            jax.ShapeDtypeStruct((tok, kv_local * HD), bf16),
            jax.ShapeDtypeStruct((tok, WIDTH), bf16),
        ],
        in_specs=[whole] * (3 * len(parts) + 7) + [pl.BlockSpec(memory_space=pl.ANY)] * 4,
        out_specs=[whole] * 3 + [pl.BlockSpec(memory_space=pl.ANY)],
        scratch_shapes=[
            vmem((tok, width), bf16),
            vmem((tok, WIDTH), bf16),
            vmem((tok, WIDTH), bf16),
            vmem((steps, HD, ROWS), f32),
            vmem((ROWS, HD), bf16),
            vmem((ROWS, HD), bf16),
            vmem((steps * (steps + 1) // 2, KT, ROWS), bf16),
            vmem((tok, WIDTH), bf16),
            vmem((tok, HD), f32),
            vmem((tok, HD), f32),
            vmem((2, tok, HD), bf16),
            vmem((kv_local, 2, tok, HD), bf16),
            vmem((2, 2, tok, HD), bf16),
            vmem((kv_local, nd, tok, HD), bf16),
            vmem((HD, tok), bf16),
            vmem((nc - 1, nd, HD, rows), bf16),
            vmem((nc - 1, nd, HD, rows), bf16),
            vmem((nd, HD, rows), f32),
            vmem((others, nd, 2, HD, rows), bf16),
            vmem((others, nd, 2, HD, rows), bf16),
            vmem((others, nd, HD, rows), bf16),
            vmem((others, nd, HD, rows), bf16),
            vmem((others, nd, 2, HD, rows), f32),
            dma((4,)),
            dma((kv_local, 2)),
            dma((kv_local, 2)),
            dma((2, 2)),
            dma((2, 2)),
            dma((kv_local, 2, nd)),
            dma((kv_local, nd)),
            dma((nc - 1, nd)),
            dma((nc - 1, nd)),
            dma((2, others, nd)),
            dma((2, others, nd)),
            dma((steps,)),
            dma((steps,)),
        ],
        compiler_params=pltpu.CompilerParams(
            collective_id=0, has_side_effects=True, vmem_limit_bytes=62 << 20),
        cost_estimate=pl.CostEstimate(
            flops=2 * tok * width * nd * kv_local * HD + 10 * 10 * KT * ROWS * HD,
            transcendentals=10 * KT * ROWS, bytes_accessed=20 << 20),
        name="tail",
    )(*[part for head in parts for part in head], *far, lse, delta, beg, k, v, q, do, dq, feat)


def finish_kernel(*refs):
    *parts, weight, value, key, dq_out, w_out, v_out, k_out = refs
    width = parts[0].shape[2]
    for i, part in enumerate(parts):
        dq_out[:, :, i * width:(i + 1) * width] = part[...]
    w_out[0] = weight[...]
    v_out[0] = value[...]
    k_out[0] = key[...]


def finish(dq_parts, weight, value, key):
    _, tok, width = dq_parts[0].shape
    n = 8
    cut = lambda a: pl.BlockSpec((a.shape[0] // n, a.shape[1]), lambda i: (i, 0))
    cut3 = lambda a: pl.BlockSpec((1, a.shape[0] // n, a.shape[1]), lambda i: (0, i, 0))
    wide = lambda w: pl.BlockSpec((1, tok // n, w), lambda i: (0, i, 0))
    return pl.pallas_call(
        finish_kernel,
        out_shape=[
            jax.ShapeDtypeStruct((1, tok, width * len(dq_parts)), jnp.bfloat16),
            jax.ShapeDtypeStruct((1, *weight.shape), weight.dtype),
            jax.ShapeDtypeStruct((1, *value.shape), value.dtype),
            jax.ShapeDtypeStruct((1, *key.shape), key.dtype),
        ],
        grid=(n,),
        in_specs=[wide(width)] * len(dq_parts) + [cut(weight), cut(value), cut(key)],
        out_specs=[wide(width * len(dq_parts)), cut3(weight), cut3(value), cut3(key)],
        compiler_params=pltpu.CompilerParams(
            dimension_semantics=("arbitrary",), vmem_limit_bytes=60 << 20),
        name="finish",
    )(*dq_parts, weight, value, key)


def weight_plain(feat, dv, nd, nc, scale):
    shard = lax.axis_index("ctx")
    rows = feat.shape[1] // nc
    dv_all = lax.all_gather(dv, "dp", axis=1, tiled=True)

    def partial(target):
        cols = lax.dynamic_slice_in_dim(feat, target * rows, rows, 1)
        return lax.dot_general(cols, dv_all, (((0,), (0,)), ((), ())),
                               preferred_element_type=jnp.float32)

    total = partial(shard)
    for by in range(1, nc):
        sent = partial((shard + by) % nc).astype(jnp.bfloat16)
        total = total + lax.ppermute(sent, "ctx", [(i, (i + by) % nc) for i in range(nc)])
    return total * scale


def local(features, queries, keys, values, attn_out, out_grad, lse, doc_starts, key_blocks):
    tok = queries.shape[1]
    kv_local = keys.shape[2] // HD
    shard = lax.axis_index("ctx")
    nc = lax.axis_size("ctx")
    nd = lax.axis_size("dp")
    ns = lax.axis_size("section")
    q, do, k, v = queries[0], out_grad[0], keys[0], values[0]

    def window(head):
        return ctx_send(packed[head], 2), ctx_send(packed[head], 1)

    packed = [jnp.concatenate([k[:, head * HD:(head + 1) * HD], v[:, head * HD:(head + 1) * HD]], axis=1)
              for head in range(kv_local)]
    windows = [window(0)]
    far, near, beg_far, beg_near = block_tables(doc_starts[0], shard, tok)
    delta, lse2 = row_tables(do, attn_out[0], lse[0])
    scale = (tok * nc) ** -0.5
    feat = features[0]
    last = kv_local - 1
    dq_parts, parts = [], []
    for head in range(last):
        dq, (own,) = attention(head, True, near, q, do, lse2, delta, beg_near, (k, v), None, False)
        packed[head + 1], _ = lax.optimization_barrier((packed[head + 1], own))
        windows.append(window(head + 1))
        dq, (two, one) = attention(head, False, far, q, do, lse2, delta, beg_far, windows[head], dq, True)
        far, _ = lax.optimization_barrier((far, two))
        dq_parts.append(home(dq, 0))
        parts.append((own, home(two, 2), home(one, 1)))
    dq, (two, one) = attention(last, False, far, q, do, lse2, delta, beg_far, windows[last], None, False)
    if nc == 4 and feat.shape[1] // nc % 128 == 0:
        weight, value_grad, key_grad, dq = tail(
            feat, q, do, k, v, lse2, delta, beg_near, parts, (two, one), dq, nd, nc, ns, scale)
        dq_parts.append(dq[None])
        query_grad, weight, value_grad, key_grad = finish(dq_parts, weight, value_grad, key_grad)
        return query_grad, key_grad, value_grad, weight
    else:
        dq, (own,) = attention(last, True, near, q, do, lse2, delta, beg_near, (k, v), dq, True)
        dq_parts.append(home(dq, 0))
        parts.append((own, home(two, 2), home(one, 1)))
        grads = [(home(own, 0).astype(jnp.float32) + two + one).astype(jnp.bfloat16) for own, two, one in parts]
        value_grad = jnp.concatenate([grad[0] for grad in grads], axis=1)
        key_grad = jnp.concatenate([grad[1] for grad in grads], axis=1)
        weight = weight_plain(feat, value_grad, nd, nc, scale)
    query_grad = jnp.concatenate(dq_parts, axis=2)
    return query_grad, key_grad[None], value_grad[None], weight[None]


def solution(mesh):
    placed = (
        P("section", "ctx", "dp"),
        P("section", "ctx", "dp"),
        P("section", "ctx", "dp"),
        P("section", "ctx", "dp"),
        P("section", "ctx", "dp"),
        P("section", "ctx", "dp"),
        P("section", "dp", "ctx"),
        P("section", None),
        P("section", "ctx", None),
    )
    return jax.shard_map(
        local,
        mesh=mesh,
        in_specs=placed,
        out_specs=(
            P("section", "ctx", "dp"),
            P("section", "ctx", "dp"),
            P("section", "ctx", "dp"),
            P("section", ("dp", "ctx"), None),
        ),
        check_vma=False,
    )
```
